32 devices in a mesh: groups: 2 (over x), rows: 16 (over z, y, core).
Axes of the slice: x: 2, y: 2, z: 4, core: 2. Of those that a mesh axis runs over, the one named last changes fastest.
Arguments:
- images: bfloat16 [32, 64, 3, 256], P('groups', 'rows'), parts along dimension 0, may hold values from -50 to 50
- shifts: int32 [32, 12], P('groups'), parts along dimension 0, may hold values from -48 to 48, as said below
- in_weight: bfloat16 [3, 3, 32, 3], replicated, may hold values from -1.25 to 1.25
- norm_gain: float32 [32], replicated, may hold values from 0.1 to 1.9
- norm_bias: float32 [32], replicated, may hold values from -3 to 3
- mid_weight: bfloat16 [3, 3, 32, 32], replicated, may hold values from -0.375 to 0.375
- out_weight: bfloat16 [3, 3, 32, 32], replicated, may hold values from -0.375 to 0.375
- cost_weight_a: bfloat16 [3, 3, 3, 32, 32], replicated, may hold values from -0.21875 to 0.21875
- cost_weight_b: bfloat16 [3, 3, 3, 32, 32], replicated, may hold values from -0.21875 to 0.21875
Outputs:
- regularized: bfloat16 [24, 64, 32, 256], P('groups', 'rows'), parts along dimension 0
The draws below stay inside these ranges and needn't reach their ends.
There are 2 independent parts, one for each index of `groups`. The reference program is written for one: setup_inputs(seed, part) draws one part's arguments, and reference() takes and returns one part's arrays. A program takes and returns all parts, laid end to end along the dimension named above; an argument that names none is the same for every part. Nothing has to cross between parts.
Inputs may be any that keep to these rules, and one draw needn't show every extreme that they name: `shifts`: the shift of camera v at plane k is b_v * (k + 1) for an integer baseline b_v of -4 to 4; some camera has b_v = 4 and another b_v = -4.
All inputs are finite; a program needn't handle non-finite values.
Results may differ from the reference program's by a relative error of at most 0.0076.
Values may be sent and summed in bfloat16 or wider, within the bound.
No kernel may reach another device: no remote copies, remote signals or barrier semaphores. Data moves between devices by JAX's collectives and lax.ppermute only.
A program may use at most 128 MiB of HBM per device.

```python
import math
import jax
import jax.numpy as jnp
from jax import lax

VIEWS = 16
C = 32
IN_CH = 3
PLANES = 12
COLS = 256
HEIGHT = 64


def draw_images(key, part):
    first_key, second_key = jax.random.split(key)
    position = jnp.arange(HEIGHT, dtype=jnp.float32) / max(HEIGHT - 1, 1)
    base = jnp.clip(jax.random.normal(first_key, (VIEWS, HEIGHT, IN_CH, COLS), jnp.float32), -4.0, 4.0)
    row_scale = jnp.exp(position * math.log(3.0))
    col_scale = jnp.exp(jax.random.uniform(second_key, (COLS,), jnp.float32, 0.0, math.log(10.0)))
    values = base * row_scale[None, :, None, None] * col_scale[None, None, None, :] / 4.0
    return values.astype(jnp.bfloat16)


def draw_shifts(key, part):
    first_key, second_key, third_key = jax.random.split(key, 3)
    baseline = jax.random.randint(first_key, (VIEWS,), -4, 5)
    first_view = jax.random.randint(second_key, (), 0, VIEWS)
    second_view = (first_view + 1 + jax.random.randint(third_key, (), 0, VIEWS - 1)) % VIEWS
    baseline = baseline.at[first_view].set(4).at[second_view].set(-4)
    steps_out = jnp.arange(PLANES, dtype=jnp.int32) + 1
    return (baseline[:, None] * steps_out[None, :]).astype(jnp.int32)


def noise(own_key, extent, deviation, limit, kind=jnp.bfloat16):
    entries = jax.random.normal(own_key, extent, jnp.float32) * deviation
    return jnp.minimum(jnp.maximum(entries, -limit), limit).astype(kind)


def setup_inputs(seed: int = 0, part: int = 0) -> dict:
    seeds = jax.random.split(jax.random.key(seed), 10)
    part_splits = jax.random.split(jax.random.fold_in(seeds[9], part), 10)
    images = draw_images(jax.random.fold_in(jax.random.fold_in(seeds[9], part), 71), part)
    shifts = draw_shifts(jax.random.fold_in(jax.random.fold_in(seeds[9], part), 71), part)
    in_weight = noise(seeds[2], (3, 3, C, IN_CH), (9 * IN_CH) ** -0.5, 1.25)
    norm_gain = jnp.clip(1.0 + 0.18 * jax.random.normal(seeds[3], (C,), jnp.float32), 0.1, 1.9)
    norm_bias = noise(seeds[4], (C,), 0.5, 3.0, jnp.float32)
    mid_weight = noise(seeds[5], (3, 3, C, C), (9 * C) ** -0.5, 0.375)
    out_weight = noise(seeds[6], (3, 3, C, C), (9 * C) ** -0.5, 0.375)
    cost_weight_a = noise(seeds[7], (3, 3, 3, C, C), (27 * C) ** -0.5, 0.21875)
    cost_weight_b = noise(seeds[8], (3, 3, 3, C, C), (27 * C) ** -0.5, 0.21875)
    return {"images": images, "shifts": shifts, "in_weight": in_weight, "norm_gain": norm_gain, "norm_bias": norm_bias, "mid_weight": mid_weight, "out_weight": out_weight, "cost_weight_a": cost_weight_a, "cost_weight_b": cost_weight_b}


def plane_conv(source, weight):
    height = source.shape[0]
    width = source.shape[2]
    padded = jnp.pad(source, ((1, 1), (0, 0), (1, 1)))
    summed = jnp.zeros((height, weight.shape[2], width), jnp.float32)
    for tap_row in range(3):
        for tap_col in range(3):
            summed = summed + jnp.einsum('oc,rcw->row', weight[tap_row, tap_col].astype(jnp.float32), padded[tap_row:tap_row + height, :, tap_col:tap_col + width], precision=lax.Precision.HIGHEST)
    return summed

def volume_conv(source, weight):
    depth = source.shape[0]
    height = source.shape[1]
    width = source.shape[3]
    padded = jnp.pad(source, ((1, 1), (1, 1), (0, 0), (1, 1)))
    summed = jnp.zeros((depth, height, weight.shape[3], width), jnp.float32)
    for tap_depth in range(3):
        for tap_row in range(3):
            for tap_col in range(3):
                summed = summed + jnp.einsum('oc,drcw->drow', weight[tap_depth, tap_row, tap_col].astype(jnp.float32), padded[tap_depth:tap_depth + depth, tap_row:tap_row + height, :, tap_col:tap_col + width], precision=lax.Precision.HIGHEST)
    return summed

def reference(images, shifts, in_weight, norm_gain, norm_bias, mid_weight, out_weight, cost_weight_a, cost_weight_b):

    def view_features(image):
        raw = plane_conv(image.astype(jnp.float32), in_weight)
        average = lax.optimization_barrier(jnp.mean(raw, axis=(0, 2)))
        centered = raw - average[None, :, None]
        spread = lax.optimization_barrier(jnp.mean(centered * centered, axis=(0, 2)))
        normed = jax.nn.relu(centered / jnp.sqrt(spread + 1e-05)[None, :, None] * norm_gain[None, :, None] + norm_bias[None, :, None]).astype(jnp.bfloat16)
        middle = jax.nn.relu(plane_conv(normed.astype(jnp.float32), mid_weight)).astype(jnp.bfloat16)
        return plane_conv(middle.astype(jnp.float32), out_weight).astype(jnp.bfloat16)
    features = lax.map(view_features, images)
    padding = 4 * PLANES
    padded = jnp.pad(features, ((0, 0), (0, 0), (0, 0), (padding, padding)))

    def one_plane(column):

        def take(view_feats, shift_by):
            return lax.dynamic_slice_in_dim(view_feats, (padding + shift_by).astype(jnp.int32), COLS, 2)
        warped = jax.vmap(take)(padded, column).astype(jnp.float32)
        average = lax.optimization_barrier(jnp.mean(warped, axis=0))
        return (lax.optimization_barrier(jnp.mean(warped * warped, axis=0)) - average * average).astype(jnp.bfloat16)
    volume = lax.map(one_plane, jnp.transpose(shifts))
    cost_hidden = jax.nn.relu(volume_conv(volume.astype(jnp.float32), cost_weight_a)).astype(jnp.bfloat16)
    return volume_conv(cost_hidden.astype(jnp.float32), cost_weight_b).astype(jnp.bfloat16)
```

```python
import functools
import jax
import jax.numpy as jnp
import numpy as np
from jax import lax
from jax.experimental import pallas as pl
from jax.experimental.pallas import tpu as pltpu
from jax.sharding import PartitionSpec as P

BF = jnp.bfloat16
F32 = jnp.float32
VMEM = pl.BlockSpec(memory_space=pltpu.VMEM)
SMEM = pl.BlockSpec(memory_space=pltpu.SMEM)
REACH = 48


def dot(a, b):
    return jnp.dot(a, b, preferred_element_type=F32)


def fold(sums):
    sums = sums + pltpu.roll(sums, 64, 1)
    return sums + pltpu.roll(sums, 32, 1)


def stats_kernel(x_ref, w_ref, pt_ref, st_ref, p_scr, t_scr, raw_scr):
    views, _, width = x_ref.shape
    lane = lax.broadcasted_iota(jnp.int32, (1, width), 1)
    p_scr[...] = jnp.zeros_like(p_scr)

    def one_view(v, carry):
        x = x_ref[v]
        before = jnp.where(lane == 0, 0.0, pltpu.roll(x, 1, 1))
        after = jnp.where(lane == width - 1, 0.0, pltpu.roll(x, width - 1, 1))
        p_scr[0:42, :] = before[0:42]
        p_scr[42:84, :] = x[0:42]
        p_scr[84:126, :] = after[0:42]
        t_scr[pl.ds(v, width, stride=views), :] = p_scr[...].T
        return carry

    lax.fori_loop(0, views, one_view, 0)
    chunk = 512
    steps = views * width // chunk

    def first(i, total):
        rows = pl.ds(pl.multiple_of(i * chunk, chunk), chunk)
        patch = t_scr[rows, :].astype(BF)
        pt_ref[rows, :] = patch
        raw = dot(patch, w_ref[...])
        raw_scr[rows, :] = raw
        return total + jnp.sum(raw.reshape(chunk // views, views, 128), axis=0)

    total = lax.fori_loop(0, steps, first, jnp.zeros((views, 128), F32))
    mean = fold(total) * (1.0 / (4 * width))

    def second(i, total):
        rows = pl.ds(pl.multiple_of(i * chunk, chunk), chunk)
        raw = raw_scr[rows, :].reshape(chunk // views, views, 128) - mean[None]
        return total + jnp.sum(raw * raw, axis=0)

    squares = lax.fori_loop(0, steps, second, jnp.zeros((views, 128), F32))
    st_ref[0:views, :] = mean
    st_ref[views:, :] = fold(squares)


def row_mask(info, first, lanes):
    row = info[0] + first + lax.broadcasted_iota(jnp.int32, (1, lanes), 1) // 32
    return jnp.where((row >= 0) & (row < info[1]), 1.0, 0.0).astype(F32)


def feature_kernel(info, pt_ref, st_ref, gb_ref, w1_ref, w2_ref, w3_ref, f_ref, nb, mid):
    views = st_ref.shape[0] // 2
    total = pt_ref.shape[0]
    size = 256
    cols = size // views
    steps = total // size
    mean = st_ref[0:views, :]
    count = (info[1] * (total // views)).astype(F32)
    scale = gb_ref[0:1, :] / jnp.sqrt(st_ref[views:, :] / count + 1e-05)
    shift = gb_ref[1:2, :]
    edge = jnp.zeros((views, 384), BF)
    nb[0:views, :] = edge
    nb[views + total :, :] = edge
    for block in range(2):
        mid[block, 0:views, :] = edge[:, :256]
        mid[block, views + total :, :] = edge[:, :256]

    def normalize(i, carry):
        rows = pl.ds(pl.multiple_of(i * size, size), size)
        out = pl.ds(pl.multiple_of(i * size + views, views), size)
        raw = dot(pt_ref[rows, :], w1_ref[...])
        for group in range(3):
            mask = row_mask(info, 4 * group - 4, 128)
            part = raw[:, group * 128 : group * 128 + 128].reshape(cols, views, 128)
            part = jnp.maximum((part - mean[None]) * scale[None] + shift[None], 0.0) * mask[None]
            nb[out, group * 128 : group * 128 + 128] = part.reshape(size, 128).astype(BF)
        return carry

    lax.fori_loop(0, steps, normalize, 0)

    def middle(i, carry):
        out = pl.ds(pl.multiple_of(i * size + views, views), size)
        for block in range(2):
            taps = [
                nb[pl.ds(pl.multiple_of(i * size + b * views, views), size), block * 128 : block * 128 + 256]
                for b in range(3)
            ]
            part = dot(jnp.concatenate(taps, axis=1), w2_ref[...])
            part = jnp.maximum(part, 0.0) * row_mask(info, 4 * block - 3, 256)
            mid[block, out, :] = part.astype(BF)
        return carry

    lax.fori_loop(0, steps, middle, 0)

    def last(i, carry):
        for block in range(2):
            taps = [mid[block, pl.ds(pl.multiple_of(i * size + b * views, views), size), :] for b in range(3)]
            part = dot(jnp.concatenate(taps, axis=1), w3_ref[...])
            part = (part * row_mask(info, 4 * block - 2, 128)).astype(BF).astype(F32)
            f_ref[pl.ds(pl.multiple_of(block * total + i * size, size), size), :] = part
        return carry

    lax.fori_loop(0, steps, last, 0)


def volume_kernel(info, base, f_ref, ca_ref, cb_ref, out_ref, s_scr, q_scr, v32, vb, hb):
    views = base.shape[0]
    planes = out_ref.shape[0]
    width = out_ref.shape[3]
    total = views * width
    s_scr[...] = jnp.zeros_like(s_scr)
    q_scr[...] = jnp.zeros_like(q_scr)
    for volume in (vb, hb):
        volume[0] = jnp.zeros_like(volume[0])
        volume[planes + 1] = jnp.zeros_like(volume[0])
    v32[...] = jnp.zeros_like(v32)

    def add_view(v, carry):
        step = base[v] + 4
        for block in range(2):
            feats = f_ref[pl.ds(block * total + v, width, stride=views), :]
            s_scr[block, step, REACH : REACH + width, :] += feats
            q_scr[block, step, REACH : REACH + width, :] += feats * feats
        return carry

    lax.fori_loop(0, views, add_view, 0)

    def spread_taps(dest, k):
        for tap in range(3):
            dest[k + 1, :, tap * 256 : tap * 256 + 256] = v32[7 + tap : 7 + tap + width, :].astype(BF)

    size = 32

    def one_plane(k, carry):
        for block in range(2):
            for part in range(width // size):
                start = REACH + part * size
                summed = s_scr[block, 4, start : start + size, :]
                squares = q_scr[block, 4, start : start + size, :]
                for step in (-4, -3, -2, -1, 1, 2, 3, 4):
                    rows = pl.ds(start + step * (k + 1), size)
                    summed = summed + s_scr[block, step + 4, rows, :]
                    squares = squares + q_scr[block, step + 4, rows, :]
                average = summed * (1.0 / views)
                value = squares * (1.0 / views) - average * average
                v32[8 + part * size : 8 + part * size + size, block * 128 : block * 128 + 128] = (
                    value.astype(BF).astype(F32)
                )
        spread_taps(vb, k)
        return carry

    lax.fori_loop(0, planes, one_plane, 0)
    mask = row_mask(info, -1, 256)

    def hidden(k, carry):
        value = dot(vb[k], ca_ref[0]) + dot(vb[k + 1], ca_ref[1]) + dot(vb[k + 2], ca_ref[2])
        v32[8 : 8 + width, :] = (jnp.maximum(value, 0.0) * mask).astype(BF).astype(F32)
        spread_taps(hb, k)
        return carry

    lax.fori_loop(0, planes, hidden, 0)

    def final(j, carry):
        k = 2 * j
        value = dot(hb[k], cb_ref[0]) + dot(hb[k + 1], cb_ref[1]) + dot(hb[k + 2], cb_ref[2]) + dot(hb[k + 3], cb_ref[3])
        out_ref[pl.ds(k, 2)] = value.T.astype(BF).reshape(2, 4, 32, width)
        return carry

    lax.fori_loop(0, planes // 2, final, 0)


def band(before, after, used):
    taps = np.zeros((3, before, after), np.float32)
    for row in range(used):
        for tap in range(3):
            taps[tap, row + tap, row] = 1.0
    return jnp.asarray(taps, BF)


def plane_band():
    taps = np.zeros((3, 4, 2), np.float32)
    for plane in range(2):
        for tap in range(3):
            taps[tap, plane + tap, plane] = 1.0
    return jnp.asarray(taps, BF)


def near(value, axis, step):
    count = lax.axis_size(axis)
    return lax.ppermute(value, axis, [(i, (i + step) % count) for i in range(count)])


def swap(value, axis, bit):
    count = lax.axis_size(axis)
    return lax.ppermute(value, axis, [(i, i ^ bit) for i in range(count)])


def merged_stats(stats, views, cells, axis):
    count = lax.axis_size(axis)
    bit = 1
    while bit < count:
        other = swap(stats, axis, bit)
        gap = stats[:views] - other[:views]
        mean = (stats[:views] + other[:views]) * 0.5
        squares = stats[views:] + other[views:] + gap * gap * (0.5 * cells * bit)
        stats = jnp.concatenate([mean, squares], axis=0)
        bit *= 2
    return stats


def shards(
    images,
    shifts,
    in_weight,
    norm_gain,
    norm_bias,
    mid_weight,
    out_weight,
    cost_weight_a,
    cost_weight_b,
):
    views, rows, colors, width = images.shape
    planes = shifts.shape[1]
    chan = in_weight.shape[2]
    count = lax.axis_size("rows")
    index = lax.axis_index("rows")
    core = index % 2
    total = views * width

    own = images.reshape(views, rows * colors, width)
    pair = swap(own, "rows", 1)
    upper = jnp.where(core == 0, own, pair)
    lower = jnp.where(core == 0, pair, own)
    both = jnp.concatenate([upper, lower], axis=1)
    halo = 5 * colors
    above = near(both[:, 2 * rows * colors - halo :], "rows", 2)
    below = near(both[:, :halo], "rows", -2)
    above = jnp.where(index < 2, jnp.zeros_like(above), above)
    below = jnp.where(index >= count - 2, jnp.zeros_like(below), below)
    around = jnp.concatenate([above, both, below], axis=1)
    kept = (rows + 10) * colors
    slab = jnp.where(core == 0, around[:, :kept], around[:, rows * colors :])
    slab = jnp.pad(slab, ((0, 0), (0, 48 - kept), (0, 0))).astype(F32)

    w1 = jnp.einsum("aboc,aqr->bqcro", in_weight, band(14, 12, 12)).reshape(3 * 14 * colors, 12 * chan)
    w1 = jnp.pad(w1, ((0, 2), (0, 0)))
    w2 = jnp.einsum("aboc,aqr->bqcro", mid_weight, band(8, 8, 6)).reshape(3 * 8 * chan, 8 * chan)
    w3 = jnp.einsum("aboc,aqr->bqcro", out_weight, band(8, 4, 4)).reshape(3 * 8 * chan, 4 * chan)
    ca = jnp.einsum("daboc,aqr->dbqcro", cost_weight_a, band(8, 8, 6)).reshape(3, 3 * 8 * chan, 8 * chan)
    cb = jnp.einsum("daboc,aqr->dbqcro", cost_weight_b, band(8, 4, 4))
    cb = jnp.einsum("dbqcro,dps->pbqcsro", cb, plane_band()).reshape(4, 3 * 8 * chan, 2 * 4 * chan)
    params = pltpu.CompilerParams(vmem_limit_bytes=60 * 1024 * 1024)

    patches, stats = pl.pallas_call(
        stats_kernel,
        name="stats",
        out_shape=(
            jax.ShapeDtypeStruct((total, 128), BF),
            jax.ShapeDtypeStruct((2 * views, 128), F32),
        ),
        in_specs=[VMEM] * 2,
        out_specs=(VMEM, VMEM),
        scratch_shapes=[pltpu.VMEM((128, width), F32), pltpu.VMEM((total, 128), F32), pltpu.VMEM((total, 128), F32)],
        compiler_params=params,
    )(slab, w1[:, 128:256])
    stats = merged_stats(stats, views, rows * width, "rows")

    info = jnp.stack([index * rows, count * rows]).astype(jnp.int32)
    gain_bias = jnp.tile(jnp.stack([norm_gain, norm_bias]), (1, 4))
    features = pl.pallas_call(
        feature_kernel,
        name="features",
        out_shape=jax.ShapeDtypeStruct((2 * total, 128), F32),
        in_specs=[SMEM] + [VMEM] * 6,
        out_specs=VMEM,
        scratch_shapes=[pltpu.VMEM((total + 2 * views, 384), BF), pltpu.VMEM((2, total + 2 * views, 256), BF)],
        compiler_params=params,
    )(info, patches, stats, gain_bias, w1, w2, w3)

    base = shifts[:, 0]
    return pl.pallas_call(
        volume_kernel,
        name="volume",
        out_shape=jax.ShapeDtypeStruct((planes, rows, chan, width), BF),
        in_specs=[SMEM, SMEM] + [VMEM] * 3,
        out_specs=VMEM,
        scratch_shapes=[
            pltpu.VMEM((2, 9, width + 2 * REACH, 128), F32),
            pltpu.VMEM((2, 9, width + 2 * REACH, 128), F32),
            pltpu.VMEM((width + 16, 256), F32),
            pltpu.VMEM((planes + 2, width, 768), BF),
            pltpu.VMEM((planes + 2, width, 768), BF),
        ],
        compiler_params=params,
    )(info, base, features, ca, cb)


def solution(mesh):
    placed = (P("groups", "rows", None, None), P("groups", None), P(), P(), P(), P(), P(), P(), P())
    return jax.shard_map(
        shards,
        mesh=mesh,
        in_specs=placed,
        out_specs=P("groups", "rows", None, None),
        check_vma=False,
    )
```

```python
import functools
import jax
import jax.numpy as jnp
from jax import lax
from jax.experimental import pallas as pl
from jax.experimental.pallas import tpu as pltpu
from jax.sharding import PartitionSpec as P

BF = jnp.bfloat16
F32 = jnp.float32
VMEM = pl.BlockSpec(memory_space=pltpu.VMEM)
SMEM = pl.BlockSpec(memory_space=pltpu.SMEM)
REACH = 48


def dot(a, b):
    return jnp.dot(a, b, preferred_element_type=F32)


def fold(sums):
    sums = sums + pltpu.roll(sums, 64, 1)
    return sums + pltpu.roll(sums, 32, 1)


def stats_kernel(both_ref, above_ref, below_ref, w_ref, pt_ref, st_ref, x_scr, p_scr, t_scr, raw_scr):
    views, tall, width = both_ref.shape
    halo = above_ref.shape[1]
    index = lax.axis_index("rows")
    core = index % 2
    top = (index >= 2).astype(F32)
    bottom = (index < lax.axis_size("rows") - 2).astype(F32)
    lane = lax.broadcasted_iota(jnp.int32, (1, width), 1)
    p_scr[...] = jnp.zeros_like(p_scr)
    x_scr[...] = jnp.zeros_like(x_scr)
    slots = p_scr.shape[0]

    def some_views(i, carry):
        for slot in range(slots):
            v = i * slots + slot
            x_scr[slot, 0:halo, :] = above_ref[v].astype(F32) * top
            x_scr[slot, halo : halo + tall, :] = both_ref[v].astype(F32)
            x_scr[slot, halo + tall : 2 * halo + tall, :] = below_ref[v].astype(F32) * bottom
            x = jnp.where(core == 0, x_scr[slot, 0:48, :], x_scr[slot, 12:60, :])
            before = jnp.where(lane == 0, 0.0, pltpu.roll(x, 1, 1))
            after = jnp.where(lane == width - 1, 0.0, pltpu.roll(x, width - 1, 1))
            p_scr[slot, 0:42, :] = before[0:42]
            p_scr[slot, 42:84, :] = x[0:42]
            p_scr[slot, 84:126, :] = after[0:42]
            t_scr[pl.ds(v, width, stride=views), :] = p_scr[slot].T
        return carry

    lax.fori_loop(0, views // slots, some_views, 0)
    chunk = 1024
    steps = views * width // chunk
    weight = w_ref[:, pl.ds(pl.multiple_of(128 - 128 * core, 128), 256)]

    def first(i, total):
        rows = pl.ds(pl.multiple_of(i * chunk, chunk), chunk)
        patch = t_scr[rows, :].astype(BF)
        pt_ref[rows, :] = patch
        raw = dot(patch, weight)
        raw_scr[rows, :] = raw
        return total + jnp.sum(raw.reshape(chunk // views, views, 256), axis=0)

    total = lax.fori_loop(0, steps, first, jnp.zeros((views, 256), F32))
    mean = fold(total[:, :128] + total[:, 128:]) * (1.0 / (8 * width))

    def second(i, total):
        rows = pl.ds(pl.multiple_of(i * chunk, chunk), chunk)
        raw = raw_scr[rows, :].reshape(chunk // views, views, 256)
        for half in range(2):
            part = raw[:, :, half * 128 : half * 128 + 128] - mean[None]
            total = total + jnp.sum(part * part, axis=0)
        return total

    squares = lax.fori_loop(0, steps, second, jnp.zeros((views, 128), F32))
    st_ref[0:views, :] = mean
    st_ref[views:, :] = fold(squares)


def row_mask(first, lanes):
    row = lax.axis_index("rows") * 4 + first + lax.broadcasted_iota(jnp.int32, (1, lanes), 1) // 32
    return jnp.where((row >= 0) & (row < lax.axis_size("rows") * 4), 1.0, 0.0).astype(F32)


def merge(one, two, views, cells):
    gap = one[:views] - two[:views]
    mean = (one[:views] + two[:views]) * 0.5
    return mean, one[views:] + two[views:] + gap * gap * (0.5 * cells)


def tiled_lanes(scr, ref):
    scr[...] = jnp.zeros_like(scr)
    scr[0:1, 0:32] = ref[...]
    return fold(scr[...])[0:1]


def main_kernel(
    shifts, pt_ref, st_ref, other_ref, gain_ref, bias_ref, w1_ref, w2_ref, w3_ref, ca_hbm, cb_hbm, out_ref,
    nb, mid, f_scr, s_scr, q_scr, v32, vb, hb, ca_ref, cb_ref, g_scr, sems,
):
    copies = [
        pltpu.make_async_copy(ca_hbm, ca_ref, sems.at[0]),
        pltpu.make_async_copy(cb_hbm, cb_ref, sems.at[1]),
    ]
    for copy in copies:
        copy.start()
    views = st_ref.shape[0] // 2
    total = pt_ref.shape[0]
    planes = out_ref.shape[0]
    width = out_ref.shape[3]
    cells = lax.axis_size("rows") * 4 * width
    mean, squares = merge(st_ref[...], other_ref[...], views, cells // 2)
    scale = tiled_lanes(g_scr, gain_ref) / jnp.sqrt(squares * (1.0 / cells) + 1e-05)
    shift = tiled_lanes(g_scr, bias_ref)
    edge = jnp.zeros((views, 384), BF)
    nb[0:views, :] = edge
    nb[views + total :, :] = edge
    for block in range(2):
        mid[block, 0:views, :] = edge[:, :256]
        mid[block, views + total :, :] = edge[:, :256]
    size = 1024
    cols = size // views
    steps = total // size
    masks = [row_mask(4 * group - 4, 128) for group in range(3)]

    def normalize(i, carry):
        rows = pl.ds(pl.multiple_of(i * size, size), size)
        out = pl.ds(pl.multiple_of(i * size + views, views), size)
        raw = dot(pt_ref[rows, :], w1_ref[...])
        for group in range(3):
            part = raw[:, group * 128 : group * 128 + 128].reshape(cols, views, 128)
            part = jnp.maximum((part - mean[None]) * scale[None] + shift[None], 0.0) * masks[group][None]
            nb[out, group * 128 : group * 128 + 128] = part.reshape(size, 128).astype(BF)
        return carry

    lax.fori_loop(0, steps, normalize, 0)
    mid_masks = [row_mask(4 * block - 3, 256) for block in range(2)]

    def middle(i, carry):
        out = pl.ds(pl.multiple_of(i * size + views, views), size)
        for block in range(2):
            taps = [
                nb[pl.ds(pl.multiple_of(i * size + b * views, views), size), block * 128 : block * 128 + 256]
                for b in range(3)
            ]
            part = dot(jnp.concatenate(taps, axis=1), w2_ref[...])
            part = jnp.maximum(part, 0.0) * mid_masks[block]
            mid[block, out, :] = part.astype(BF)
        return carry

    lax.fori_loop(0, steps, middle, 0)
    last_masks = [row_mask(4 * block - 2, 128) for block in range(2)]
    couples = 32

    def last(i, carry):
        for block in range(2):
            rows = pl.ds(pl.multiple_of(i * couples * 2 * views, 2 * views), (couples + 1) * 2 * views)
            value = mid[block, rows, :].reshape(couples + 1, 2, views, 256)
            taps = [value[j // 2 : j // 2 + couples, j % 2].reshape(couples * views, 256) for j in range(4)]
            part = dot(jnp.concatenate(taps, axis=1), w3_ref[...])
            halves = [
                (part[:, q * 128 : q * 128 + 128] * last_masks[block]).astype(BF).astype(F32).reshape(couples, 1, views, 128)
                for q in range(2)
            ]
            start = pl.multiple_of(block * total + i * couples * 2 * views, 2 * views)
            f_scr[pl.ds(start, couples * 2 * views), :] = jnp.concatenate(halves, axis=1).reshape(couples * 2 * views, 128)
        return carry

    lax.fori_loop(0, width // 2 // couples, last, 0)

    s_scr[...] = jnp.zeros_like(s_scr)
    q_scr[...] = jnp.zeros_like(q_scr)
    for pair in (0, planes // 2):
        hb[pair, pair * 2 // planes] = jnp.zeros_like(hb[0, 0])
    vb[0] = jnp.zeros_like(vb[0])
    vb[planes + 1] = jnp.zeros_like(vb[0])
    v32[...] = jnp.zeros_like(v32)

    def add_view(v, carry):
        step = shifts[v, 0] + 4
        for block in range(2):
            feats = f_scr[pl.ds(block * total + v, width, stride=views), :]
            s_scr[block, step, REACH : REACH + width, :] += feats
            q_scr[block, step, REACH : REACH + width, :] += feats * feats
        return carry

    lax.fori_loop(0, views, add_view, 0)
    part_size = 32

    def one_plane(k, carry):
        for block in range(2):
            for part in range(width // part_size):
                start = REACH + part * part_size
                summed = s_scr[block, 4, start : start + part_size, :]
                squares = q_scr[block, 4, start : start + part_size, :]
                for step in (-4, -3, -2, -1, 1, 2, 3, 4):
                    rows = pl.ds(start + step * (k + 1), part_size)
                    summed = summed + s_scr[block, step + 4, rows, :]
                    squares = squares + q_scr[block, step + 4, rows, :]
                average = summed * (1.0 / views)
                value = (squares * (1.0 / views) - average * average).astype(BF)
                v32[0, 8 + part * part_size : 8 + part * part_size + part_size, block * 128 : block * 128 + 128] = (
                    value.astype(F32)
                )
        for tap in range(3):
            vb[k + 1, :, tap * 256 : tap * 256 + 256] = v32[0, 7 + tap : 7 + tap + width, :].astype(BF)
        return carry

    lax.fori_loop(0, planes, one_plane, 0)
    mask = row_mask(-1, 256)
    group = v32.shape[0]
    copies[0].wait()

    def hidden(i, carry):
        k = i * group
        value = sum(dot(vb[pl.ds(k + d, group)].reshape(group * width, 768), ca_ref[d]) for d in range(3))
        value = (jnp.maximum(value, 0.0) * mask).astype(BF).astype(F32)
        for t in range(group):
            v32[t, 8 : 8 + width, :] = value[t * width : (t + 1) * width]
            plane = k + t + 1
            for tap in range(3):
                hb[plane // 2, plane % 2, :, tap * 256 : tap * 256 + 256] = v32[t, 7 + tap : 7 + tap + width, :].astype(BF)
        return carry

    lax.fori_loop(0, planes // group, hidden, 0)
    pairs = 3
    copies[1].wait()

    def final(i, carry):
        j = i * pairs
        value = sum(
            dot(hb[pl.ds(j + p // 2, pairs), p % 2].reshape(pairs * width, 768), cb_ref[p]) for p in range(4)
        )
        for t in range(pairs):
            part = value[t * width : (t + 1) * width].T
            out_ref[pl.ds(2 * (j + t), 2)] = part.astype(BF).reshape(2, 4, 32, width)
        return carry

    lax.fori_loop(0, planes // 2 // pairs, final, 0)


def one_hot(rows, lanes, same):
    row = lax.broadcasted_iota(jnp.int32, (rows, lanes), 0)
    lane = lax.broadcasted_iota(jnp.int32, (rows, lanes), 1)
    return jnp.where(same(row, lane), 1.0, 0.0)


def tiled_blocks(w_ref, index, eye):
    return [
        lax.dot_general(w_ref[index(a)], eye, (((0,), (0,)), ((), ())), preferred_element_type=F32) for a in range(3)
    ]


def banded(blocks, row_in, used):
    group = lax.broadcasted_iota(jnp.int32, blocks[0].shape, 1) // 32
    value = jnp.zeros_like(blocks[0])
    for a in range(3):
        if 0 <= row_in - a < used:
            value = jnp.where(group == row_in - a, blocks[a], value)
    return value.astype(BF)


def small_weights_kernel(win_ref, wmid_ref, wout_ref, w1_ref, w2_ref, w3_ref):
    eye = one_hot(32, 384, lambda row, lane: row == lane % 32).astype(BF)
    colors = dot(win_ref[...], eye).astype(BF)
    value = jnp.zeros((128, 384), F32)
    row = lax.broadcasted_iota(jnp.int32, (128, 384), 0)
    group = lax.broadcasted_iota(jnp.int32, (128, 384), 1) // 32
    for a in range(3):
        pick = one_hot(128, 32, lambda row, lane: (lane == 9 * a + 3 * (row // 42) + row % 3) & (row < 126)).astype(BF)
        value = jnp.where(group == (row % 42) // 3 - a, dot(pick, colors), value)
    w1_ref[...] = value.astype(BF)
    for b in range(3):
        blocks = tiled_blocks(wmid_ref, lambda a: 3 * a + b, eye[:, :256])
        for row_in in range(8):
            start = b * 256 + row_in * 32
            w2_ref[start : start + 32, :] = banded(blocks, row_in, 6)
        blocks = tiled_blocks(wout_ref, lambda a: 3 * a + b, eye[:, :128])
        for row_in in range(8):
            value = banded(blocks, row_in, 4)
            for q in range(2):
                start = (b + q) * 256 + row_in * 32
                w3_ref[start : start + 32, q * 128 : q * 128 + 128] = value
    w3_ref[0:256, 128:256] = jnp.zeros((256, 128), BF)
    w3_ref[768:1024, 0:128] = jnp.zeros((256, 128), BF)


def cost_weights_kernel(wa_ref, wb_ref, ca_ref, cb_ref):
    eye = one_hot(32, 256, lambda row, lane: row == lane % 32).astype(BF)
    blank = jnp.zeros((768, 128), BF)
    cb_ref[0, :, 128:256] = blank
    cb_ref[3, :, 0:128] = blank
    for plane in range(3):
        for e in range(3):
            blocks = tiled_blocks(wa_ref, lambda a: 9 * plane + 3 * a + e, eye)
            for row_in in range(8):
                start = e * 256 + row_in * 32
                ca_ref[plane, start : start + 32, :] = banded(blocks, row_in, 6)
            blocks = tiled_blocks(wb_ref, lambda a: 9 * plane + 3 * a + e, eye[:, :128])
            for row_in in range(8):
                start = e * 256 + row_in * 32
                value = banded(blocks, row_in, 4)
                cb_ref[plane, start : start + 32, 0:128] = value
                cb_ref[plane + 1, start : start + 32, 128:256] = value


def near(value, axis, step):
    count = lax.axis_size(axis)
    return lax.ppermute(value, axis, [(i, (i + step) % count) for i in range(count)])


def swap(value, axis, bit):
    count = lax.axis_size(axis)
    return lax.ppermute(value, axis, [(i, i ^ bit) for i in range(count)])


def shards(
    images,
    shifts,
    in_weight,
    norm_gain,
    norm_bias,
    mid_weight,
    out_weight,
    cost_weight_a,
    cost_weight_b,
):
    views, rows, colors, width = images.shape
    planes = shifts.shape[1]
    chan = in_weight.shape[2]
    count = lax.axis_size("rows")
    index = lax.axis_index("rows")
    core = index % 2
    total = views * width

    own = images.reshape(views, rows * colors, width)
    pair = swap(own, "rows", 1)
    upper = jnp.where(core == 0, own, pair)
    lower = jnp.where(core == 0, pair, own)
    both = jnp.concatenate([upper, lower], axis=1)
    halo = 5 * colors
    above = near(both[:, 2 * rows * colors - halo :], "rows", 2)
    below = near(both[:, :halo], "rows", -2)

    params = pltpu.CompilerParams(vmem_limit_bytes=60 * 1024 * 1024)

    colors_in = in_weight.transpose(0, 1, 3, 2).reshape(9 * colors, chan)
    colors_in = jnp.pad(colors_in, ((0, 32 - 9 * colors), (0, 0)))
    w1, w2, w3 = pl.pallas_call(
        small_weights_kernel,
        name="small_weights",
        out_shape=(
            jax.ShapeDtypeStruct((128, 384), BF),
            jax.ShapeDtypeStruct((768, 256), BF),
            jax.ShapeDtypeStruct((1024, 256), BF),
        ),
        in_specs=[VMEM] * 3,
        out_specs=(VMEM,) * 3,
        cost_estimate=pl.CostEstimate(flops=2000000, bytes_accessed=1000000, transcendentals=0),
    )(colors_in, mid_weight.reshape(9, chan, chan), out_weight.reshape(9, chan, chan))
    ca, cb = pl.pallas_call(
        cost_weights_kernel,
        name="cost_weights",
        out_shape=(jax.ShapeDtypeStruct((3, 768, 256), BF), jax.ShapeDtypeStruct((4, 768, 256), BF)),
        in_specs=[VMEM] * 2,
        out_specs=(VMEM,) * 2,
        cost_estimate=pl.CostEstimate(flops=2000000, bytes_accessed=3500000, transcendentals=0),
        compiler_params=params,
    )(cost_weight_a.reshape(27, chan, chan), cost_weight_b.reshape(27, chan, chan))

    patches, stats = pl.pallas_call(
        stats_kernel,
        name="stats",
        out_shape=(
            jax.ShapeDtypeStruct((total, 128), BF),
            jax.ShapeDtypeStruct((2 * views, 128), F32),
        ),
        in_specs=[VMEM] * 4,
        out_specs=(VMEM, VMEM),
        scratch_shapes=[
            pltpu.VMEM((4, 64, width), F32),
            pltpu.VMEM((4, 128, width), F32),
            pltpu.VMEM((total, 128), F32),
            pltpu.VMEM((total, 256), F32),
        ],
        compiler_params=params,
    )(both, above, below, w1)
    bit = 2
    while True:
        other = swap(stats, "rows", bit)
        if 2 * bit >= count:
            break
        stats = jnp.concatenate(merge(stats, other, views, rows * width * bit), axis=0)
        bit *= 2

    return pl.pallas_call(
        main_kernel,
        name="main",
        out_shape=jax.ShapeDtypeStruct((planes, rows, chan, width), BF),
        in_specs=[SMEM] + [VMEM] * 8 + [pl.BlockSpec(memory_space=pl.ANY)] * 2,
        out_specs=VMEM,
        scratch_shapes=[
            pltpu.VMEM((total + 2 * views, 384), BF),
            pltpu.VMEM((2, total + 2 * views, 256), BF),
            pltpu.VMEM((2 * total, 128), F32),
            pltpu.VMEM((2, 9, width + 2 * REACH, 128), F32),
            pltpu.VMEM((2, 9, width + 2 * REACH, 128), F32),
            pltpu.VMEM((4, width + 16, 256), F32),
            pltpu.VMEM((planes + 2, width, 768), BF),
            pltpu.VMEM((planes // 2 + 1, 2, width, 768), BF),
            pltpu.VMEM((3, 768, 256), BF),
            pltpu.VMEM((4, 768, 256), BF),
            pltpu.VMEM((8, 128), F32),
            pltpu.SemaphoreType.DMA((2,)),
        ],
        compiler_params=params,
    )(shifts, patches, stats, other, norm_gain[None], norm_bias[None], w1, w2, w3, ca, cb)


def solution(mesh):
    placed = (P("groups", "rows", None, None), P("groups", None), P(), P(), P(), P(), P(), P(), P())
    return jax.shard_map(
        shards,
        mesh=mesh,
        in_specs=placed,
        out_specs=P("groups", "rows", None, None),
        check_vma=False,
    )
```

```python
import functools
import jax
import jax.numpy as jnp
import numpy as np
from jax import lax
from jax.experimental import pallas as pl
from jax.experimental.pallas import tpu as pltpu
from jax.sharding import PartitionSpec as P

BF = jnp.bfloat16
F32 = jnp.float32
VMEM = pl.BlockSpec(memory_space=pltpu.VMEM)
SMEM = pl.BlockSpec(memory_space=pltpu.SMEM)
REACH = 48


def dot(a, b):
    return jnp.dot(a, b, preferred_element_type=F32)


def fold(sums):
    sums = sums + pltpu.roll(sums, 64, 1)
    return sums + pltpu.roll(sums, 32, 1)


def stats_kernel(own_ref, pair_ref, far_ref, near_ref, next_ref, w_ref, pt_ref, st_ref, x_scr, p_scr, t_scr):
    views, tall, width = own_ref.shape
    index = lax.axis_index("rows")
    first_core = index % 2 == 0
    top = (index >= 2).astype(F32)
    bottom = (index < lax.axis_size("rows") - 2).astype(F32)
    beyond = jnp.where(first_core, top, bottom)
    lane = lax.broadcasted_iota(jnp.int32, (1, width), 1)
    p_scr[...] = jnp.zeros_like(p_scr)
    slots = p_scr.shape[0]

    def some_views(i, carry):
        for slot in range(slots):
            v = i * slots + slot
            pair = pair_ref[v].astype(F32)
            far = far_ref[v].astype(F32) * beyond
            one = near_ref[v].astype(F32)
            two = next_ref[v].astype(F32)
            x_scr[slot, 0:3, :] = jnp.where(first_core, one, two) * top
            x_scr[slot, 3:15, :] = jnp.where(first_core, far, pair)
            x_scr[slot, 15:27, :] = own_ref[v].astype(F32)
            x_scr[slot, 27:39, :] = jnp.where(first_core, pair, far)
            x_scr[slot, 39:42, :] = jnp.where(first_core, two, one) * bottom
            x = x_scr[slot, 0:42, :]
            p_scr[slot, 0:42, :] = jnp.where(lane == 0, 0.0, pltpu.roll(x, 1, 1))
            p_scr[slot, 42:84, :] = x
            p_scr[slot, 84:126, :] = jnp.where(lane == width - 1, 0.0, pltpu.roll(x, width - 1, 1))
            t_scr[pl.ds(v, width, stride=views), :] = p_scr[slot].T
        return carry

    lax.fori_loop(0, views // slots, some_views, 0)
    chunk = 1024
    steps = views * width // chunk
    weight = w_ref[:, pl.ds(pl.multiple_of(jnp.where(first_core, 128, 0), 128), 256)]
    center = None
    total = squares = 0.0
    for i in range(steps):
        rows = slice(i * chunk, (i + 1) * chunk)
        patch = t_scr[rows, :].astype(BF)
        pt_ref[rows, :] = patch
        raw = dot(patch, weight).reshape(chunk // views, views, 256)
        if center is None:
            start = jnp.sum(raw, axis=0)
            center = fold(start[:, :128] + start[:, 128:]) * (1.0 / (8 * chunk // views))
        for half in range(2):
            part = raw[:, :, half * 128 : half * 128 + 128] - center[None]
            total = total + jnp.sum(part, axis=0)
            squares = squares + jnp.sum(part * part, axis=0)
    offset = fold(total) * (1.0 / (8 * width))
    st_ref[0:views, :] = center + offset
    st_ref[views:, :] = fold(squares) - offset * offset * (8.0 * width)


def row_mask(first, lanes):
    row = lax.axis_index("rows") * 4 + first + (lax.broadcasted_iota(jnp.int32, (1, lanes), 1) >> 5)
    return jnp.where((row >= 0) & (row < lax.axis_size("rows") * 4), 1.0, 0.0).astype(F32)


def merge(one, two, views, cells):
    gap = one[:views] - two[:views]
    mean = (one[:views] + two[:views]) * 0.5
    return mean, one[views:] + two[views:] + gap * gap * (0.5 * cells)


def tiled_lanes(scr, ref):
    scr[...] = jnp.zeros_like(scr)
    scr[0:1, 0:32] = ref[...]
    return fold(scr[...])[0:1]


def main_kernel(
    shifts, pt_ref, st_ref, other_ref, gain_ref, bias_ref, w1_ref, w2_ref, w3_ref, ca_hbm, cb_hbm, out_ref,
    nb, mid, f_scr, s_low, s_high, q_low, q_high, v32, vb, hb, ca_ref, cb_ref, g_scr, sems,
):
    copies = [
        pltpu.make_async_copy(ca_hbm, ca_ref, sems.at[0]),
        pltpu.make_async_copy(cb_hbm, cb_ref, sems.at[1]),
    ]
    for copy in copies:
        copy.start()
    s_scr, q_scr = (s_low, s_high), (q_low, q_high)
    views = st_ref.shape[0] // 2
    total = pt_ref.shape[0]
    planes = out_ref.shape[0]
    width = out_ref.shape[3]
    cells = lax.axis_size("rows") * 4 * width
    mean, squares = merge(st_ref[...], other_ref[...], views, cells // 2)
    scale = tiled_lanes(g_scr, gain_ref) / jnp.sqrt(squares * (1.0 / cells) + 1e-05)
    shift = tiled_lanes(g_scr, bias_ref)
    edge = jnp.zeros((views, 384), BF)
    nb[0:views, :] = edge
    nb[views + total :, :] = edge
    for block in range(2):
        mid[block, 0:views, :] = edge[:, :256]
        mid[block, views + total :, :] = edge[:, :256]
    size = 1024
    cols = size // views
    steps = total // size
    masks = [row_mask(4 * group - 4, 128) for group in range(3)]

    def normalize(i, carry):
        rows = pl.ds(pl.multiple_of(i * size, size), size)
        out = pl.ds(pl.multiple_of(i * size + views, views), size)
        raw = dot(pt_ref[rows, :], w1_ref[...])
        for group in range(3):
            part = raw[:, group * 128 : group * 128 + 128].reshape(cols, views, 128)
            part = jnp.maximum((part - mean[None]) * scale[None] + shift[None], 0.0) * masks[group][None]
            nb[out, group * 128 : group * 128 + 128] = part.reshape(size, 128).astype(BF)
        return carry

    mid_masks = [row_mask(4 * block - 3, 256) for block in range(2)]

    def middle(i, carry):
        out = pl.ds(pl.multiple_of(i * size + views, views), size)
        for block in range(2):
            taps = [
                nb[pl.ds(pl.multiple_of(i * size + b * views, views), size), block * 128 : block * 128 + 256]
                for b in range(3)
            ]
            part = dot(jnp.concatenate(taps, axis=1), w2_ref[...])
            part = jnp.maximum(part, 0.0) * mid_masks[block]
            mid[block, out, :] = part.astype(BF)
        return carry

    last_masks = [row_mask(4 * block - 2, 128) for block in range(2)]
    couples = 32
    apart = 17

    def last(i, carry):
        for block in range(2):
            rows = pl.ds(i * couples * 2 * views, (couples + 1) * 2 * views)
            value = mid[block, rows, :].reshape(couples + 1, 2, views, 256)
            taps = [value[j // 2 : j // 2 + couples, j % 2].reshape(couples * views, 256) for j in range(4)]
            part = dot(jnp.concatenate(taps, axis=1), w3_ref[...])
            for q in range(2):
                half = (part[:, q * 128 : q * 128 + 128] * last_masks[block]).astype(BF).astype(F32)
                for m in range(couples):
                    start = (block * width + (i * couples + m) * 2 + q) * apart
                    f_scr[start : start + views, :] = half[m * views : (m + 1) * views]

    for ref in s_scr + q_scr:
        ref[...] = jnp.zeros_like(ref)

    def add_views(i):
        for v in range(views):
            step = shifts[v, 0] + 4
            for block in range(2):
                feats = f_scr[pl.ds((block * width + i * cols) * apart + v, cols, stride=apart), :]
                s_scr[block][step, REACH + i * cols : REACH + (i + 1) * cols, :] += feats
                q_scr[block][step, REACH + i * cols : REACH + (i + 1) * cols, :] += feats * feats

    for i in range(steps + 3):
        if i < steps:
            normalize(i, 0)
        if 0 <= i - 1 < steps:
            middle(i - 1, 0)
        if 0 <= i - 2 < steps:
            last(i - 2, 0)
        if 0 <= i - 3 < steps:
            add_views(i - 3)

    for pair in (0, planes // 2):
        hb[pair, pair * 2 // planes] = jnp.zeros_like(hb[0, 0])
    vb[0] = jnp.zeros_like(vb[0])
    vb[planes + 1] = jnp.zeros_like(vb[0])
    v32[...] = jnp.zeros_like(v32)

    part_size = 32

    def one_plane(k, carry):
        for block in range(2):
            for part in range(width // part_size):
                start = REACH + part * part_size
                summed = s_scr[block][4, start : start + part_size, :]
                squares = q_scr[block][4, start : start + part_size, :]
                for step in (-4, -3, -2, -1, 1, 2, 3, 4):
                    rows = pl.ds(start + step * (k + 1), part_size)
                    summed = summed + s_scr[block][step + 4, rows, :]
                    squares = squares + q_scr[block][step + 4, rows, :]
                average = summed * (1.0 / views)
                value = (squares * (1.0 / views) - average * average).astype(BF)
                v32[k % 4, 8 + part * part_size : 8 + part * part_size + part_size, block * 128 : block * 128 + 128] = (
                    value.astype(F32)
                )
        for tap in range(3):
            vb[k + 1, :, tap * 256 : tap * 256 + 256] = v32[k % 4, 7 + tap : 7 + tap + width, :].astype(BF)
        return carry

    mask = row_mask(-1, 256)
    group = 2

    def hidden(i, carry):
        k = i * group
        value = dot(jnp.concatenate([vb[pl.ds(k + d, group)].reshape(group * width, 768) for d in range(3)], axis=1), ca_ref[...].reshape(2304, 256))
        value = (jnp.maximum(value, 0.0) * mask).astype(BF).astype(F32)
        for t in range(group):
            v32[4 + 2 * (i % 2) + t, 8 : 8 + width, :] = value[t * width : (t + 1) * width]
            plane = k + t + 1
            for tap in range(3):
                hb[plane // 2, plane % 2, :, tap * 256 : tap * 256 + 256] = v32[4 + 2 * (i % 2) + t, 7 + tap : 7 + tap + width, :].astype(BF)
        return carry

    pairs = 3

    def final(i, carry):
        j = i * pairs
        taps = [hb[pl.ds(j + p // 2, pairs), p % 2].reshape(pairs * width, 768) for p in range(4)]
        value = dot(jnp.concatenate(taps, axis=1), cb_ref[...].reshape(3072, 256))
        for t in range(pairs):
            part = value[t * width : (t + 1) * width].T
            out_ref[pl.ds(2 * (j + t), 2)] = part.astype(BF).reshape(2, 4, 32, width)
        return carry

    for copy in copies:
        copy.wait()
    for k in range(4):
        one_plane(k, 0)
    for i in range(6):
        hidden(i, 0)
        if i < 4:
            one_plane(2 * i + 4, 0)
            one_plane(2 * i + 5, 0)
    final(0, 0)
    final(1, 0)


def one_hot(rows, lanes, same):
    row = lax.broadcasted_iota(jnp.int32, (rows, lanes), 0)
    lane = lax.broadcasted_iota(jnp.int32, (rows, lanes), 1)
    return jnp.where(same(row, lane), 1.0, 0.0)


def tiled_blocks(w_ref, index, eye):
    return [
        lax.dot_general(w_ref[index(a)], eye, (((0,), (0,)), ((), ())), preferred_element_type=F32) for a in range(3)
    ]


def banded(blocks, row_in, used):
    group = lax.broadcasted_iota(jnp.int32, blocks[0].shape, 1) >> 5
    value = jnp.zeros_like(blocks[0])
    for a in range(3):
        if 0 <= row_in - a < used:
            value = jnp.where(group == row_in - a, blocks[a], value)
    return value.astype(BF)


def color_weights_kernel(w_ref, pick_ref, tap_ref, w1_ref):
    eye = one_hot(32, 384, lambda row, lane: row == (lane & 31)).astype(BF)
    colors = dot(w_ref[...], eye).astype(BF)
    picked = dot(pick_ref[...], colors)
    taps = tap_ref[...]
    value = jnp.zeros((128, 384), F32)
    for a in range(3):
        value = jnp.where(taps == a, picked[a * 128 : a * 128 + 128], value)
    w1_ref[...] = value.astype(BF)


def color_places(rows_in, rows_out):
    pick = np.zeros((3, 128, 27), np.float32)
    taps = np.full((128, rows_out, 32), 3, np.int32)
    for b in range(3):
        for row in range(rows_in):
            for c in range(3):
                place = (b * rows_in + row) * 3 + c
                for a in range(3):
                    pick[a, place, 9 * a + 3 * b + c] = 1.0
                    if 0 <= row - a < rows_out:
                        taps[place, row - a] = a
    return jnp.asarray(pick.reshape(384, 27), BF), jnp.asarray(taps.reshape(128, rows_out * 32))


def feature_weights_kernel(wmid_ref, wout_ref, w2_ref, w3_ref):
    eye = one_hot(32, 256, lambda row, lane: row == (lane & 31)).astype(BF)
    for b in range(3):
        blocks = tiled_blocks(wmid_ref, lambda a: 3 * a + b, eye)
        for row_in in range(8):
            start = b * 256 + row_in * 32
            w2_ref[start : start + 32, :] = banded(blocks, row_in, 6)
        blocks = tiled_blocks(wout_ref, lambda a: 3 * a + b, eye[:, :128])
        for row_in in range(8):
            value = banded(blocks, row_in, 4)
            for q in range(2):
                start = (b + q) * 256 + row_in * 32
                w3_ref[start : start + 32, q * 128 : q * 128 + 128] = value
    w3_ref[0:256, 128:256] = jnp.zeros((256, 128), BF)
    w3_ref[768:1024, 0:128] = jnp.zeros((256, 128), BF)


def hidden_weights_kernel(w_ref, ca_ref):
    eye = one_hot(32, 256, lambda row, lane: row == (lane & 31)).astype(BF)
    for plane in range(3):
        for e in range(3):
            blocks = tiled_blocks(w_ref, lambda a: 9 * plane + 3 * a + e, eye)
            for row_in in range(8):
                start = e * 256 + row_in * 32
                ca_ref[plane, start : start + 32, :] = banded(blocks, row_in, 6)


def final_weights_kernel(w_ref, cb_ref):
    eye = one_hot(32, 128, lambda row, lane: row == (lane & 31)).astype(BF)
    blank = jnp.zeros((768, 128), BF)
    cb_ref[0, :, 128:256] = blank
    cb_ref[3, :, 0:128] = blank
    for plane in range(3):
        for e in range(3):
            blocks = tiled_blocks(w_ref, lambda a: 9 * plane + 3 * a + e, eye)
            for row_in in range(8):
                start = e * 256 + row_in * 32
                value = banded(blocks, row_in, 4)
                cb_ref[plane, start : start + 32, 0:128] = value
                cb_ref[plane + 1, start : start + 32, 128:256] = value


def send(value, axis, even, odd):
    count = lax.axis_size(axis)
    pairs = []
    for i in range(count):
        to = i + (odd if i % 2 else even)
        if not 0 <= to < count:
            to = i ^ 1 if abs(even) == 2 else i
        pairs.append((i, to))
    return lax.ppermute(value, axis, pairs)


def swap(value, axis, bit):
    count = lax.axis_size(axis)
    return lax.ppermute(value, axis, [(i, i ^ bit) for i in range(count)])


def limit(mib):
    return pltpu.CompilerParams(vmem_limit_bytes=mib * 1024 * 1024)


def shards(
    images,
    shifts,
    in_weight,
    norm_gain,
    norm_bias,
    mid_weight,
    out_weight,
    cost_weight_a,
    cost_weight_b,
):
    views, rows, colors, width = images.shape
    planes = shifts.shape[1]
    chan = in_weight.shape[2]
    count = lax.axis_size("rows")
    index = lax.axis_index("rows")
    core = index % 2
    total = views * width


    def weights(kernel, shapes, *operands):
        shapes = tuple(jax.ShapeDtypeStruct(shape, BF) for shape in shapes)
        size = 2 * sum(shape.size for shape in shapes)
        return pl.pallas_call(
            kernel,
            name=kernel.__name__,
            out_shape=shapes,
            in_specs=[VMEM] * len(operands),
            out_specs=(VMEM,) * len(shapes),
            cost_estimate=pl.CostEstimate(flops=size, bytes_accessed=2 * size, transcendentals=0),
            compiler_params=limit(8),
        )(*operands)

    own = images.reshape(views, rows * colors, width)
    head, tail = own[:, :colors], own[:, (rows - 1) * colors :]
    pair = swap(own, "rows", 1)
    far = send(own, "rows", -1, 1)
    near = send(jnp.where(core == 0, tail, head), "rows", 2, -2)
    after = send(jnp.where(core == 0, head, tail), "rows", -2, 2)
    colors_in = in_weight.transpose(0, 1, 3, 2).reshape(9 * colors, chan)
    (w1,) = weights(color_weights_kernel, [(128, 384)], colors_in, *color_places(rows + 10, rows + 8))

    patches, stats = pl.pallas_call(
        stats_kernel,
        name="stats",
        out_shape=(
            jax.ShapeDtypeStruct((total, 128), BF),
            jax.ShapeDtypeStruct((2 * views, 128), F32),
        ),
        in_specs=[VMEM] * 6,
        out_specs=(VMEM, VMEM),
        scratch_shapes=[
            pltpu.VMEM((4, 48, width), F32),
            pltpu.VMEM((4, 128, width), F32),
            pltpu.VMEM((total, 128), F32),
        ],
        compiler_params=limit(12),
    )(own, pair, far, near, after, w1)
    jobs = [
        (feature_weights_kernel, [(768, 256), (1024, 256)], (mid_weight.reshape(9, chan, chan), out_weight.reshape(9, chan, chan))),
        (hidden_weights_kernel, [(3, 768, 256)], (cost_weight_a.reshape(27, chan, chan),)),
        (final_weights_kernel, [(4, 768, 256)], (cost_weight_b.reshape(27, chan, chan),)),
    ]
    made = []
    bit = 2
    while True:
        last = 2 * bit >= count
        other = swap(stats, "rows", bit)
        while jobs:
            kernel, shapes, operands = jobs.pop(0)
            stats, operands = lax.optimization_barrier((stats, operands))
            new = weights(kernel, shapes, *operands)
            if not last:
                other, new = lax.optimization_barrier((other, new))
            made.extend(new)
            if not last:
                break
        if last:
            break
        stats = jnp.concatenate(merge(stats, other, views, rows * width * bit), axis=0)
        bit *= 2
    w2, w3, ca, cb = made

    return pl.pallas_call(
        main_kernel,
        name="main",
        out_shape=jax.ShapeDtypeStruct((planes, rows, chan, width), BF),
        in_specs=[SMEM] + [VMEM] * 8 + [pl.BlockSpec(memory_space=pl.ANY)] * 2,
        out_specs=VMEM,
        scratch_shapes=[
            pltpu.VMEM((total + 2 * views, 384), BF),
            pltpu.VMEM((2, total + 2 * views, 256), BF),
            pltpu.VMEM((2 * width * 17, 128), F32),
            *[pltpu.VMEM((9, width + 2 * REACH, 128), F32) for _ in range(4)],
            pltpu.VMEM((8, width + 16, 256), F32),
            pltpu.VMEM((planes + 2, width, 768), BF),
            pltpu.VMEM((planes // 2 + 1, 2, width, 768), BF),
            pltpu.VMEM((3, 768, 256), BF),
            pltpu.VMEM((4, 768, 256), BF),
            pltpu.VMEM((8, 128), F32),
            pltpu.SemaphoreType.DMA((2,)),
        ],
        compiler_params=limit(44),
    )(shifts, patches, stats, other, norm_gain[None], norm_bias[None], w1, w2, w3, ca, cb)


def solution(mesh):
    placed = (P("groups", "rows", None, None), P("groups", None), P(), P(), P(), P(), P(), P(), P())
    return jax.shard_map(
        shards,
        mesh=mesh,
        in_specs=placed,
        out_specs=P("groups", "rows", None, None),
        check_vma=False,
    )
```

```python
import functools
import jax
import jax.numpy as jnp
from jax import lax
from jax.experimental import pallas as pl
from jax.experimental.pallas import tpu as pltpu
from jax.sharding import PartitionSpec as P

BF = jnp.bfloat16
F32 = jnp.float32
VMEM = pl.BlockSpec(memory_space=pltpu.VMEM)
SMEM = pl.BlockSpec(memory_space=pltpu.SMEM)
REACH = 48


def dot(a, b):
    return jnp.dot(a, b, preferred_element_type=F32)


def fold(sums):
    sums = sums + pltpu.roll(sums, 64, 1)
    return sums + pltpu.roll(sums, 32, 1)


def stats_kernel(own_ref, pair_ref, far_ref, near_ref, next_ref, w_ref, pt_ref, st_ref, x_scr, p_scr, t_scr):
    views, tall, width = own_ref.shape
    index = lax.axis_index("rows")
    first_core = index % 2 == 0
    top = (index >= 2).astype(F32)
    bottom = (index < lax.axis_size("rows") - 2).astype(F32)
    beyond = jnp.where(first_core, top, bottom)
    lane = lax.broadcasted_iota(jnp.int32, (1, width), 1)
    p_scr[...] = jnp.zeros_like(p_scr)
    slots = p_scr.shape[0]
    apart = views + 1

    def some_views(i, carry):
        for slot in range(slots):
            v = i * slots + slot
            pair = pair_ref[v].astype(F32)
            far = far_ref[v].astype(F32) * beyond
            one = near_ref[v].astype(F32)
            two = next_ref[v].astype(F32)
            x_scr[slot, 0:3, :] = jnp.where(first_core, one, two) * top
            x_scr[slot, 3:15, :] = jnp.where(first_core, far, pair)
            x_scr[slot, 15:27, :] = own_ref[v].astype(F32)
            x_scr[slot, 27:39, :] = jnp.where(first_core, pair, far)
            x_scr[slot, 39:42, :] = jnp.where(first_core, two, one) * bottom
            x = x_scr[slot, 0:42, :]
            p_scr[slot, 0:42, :] = jnp.where(lane == 0, 0.0, pltpu.roll(x, 1, 1))
            p_scr[slot, 42:84, :] = x
            p_scr[slot, 84:126, :] = jnp.where(lane == width - 1, 0.0, pltpu.roll(x, width - 1, 1))
            t_scr[pl.ds(v, width, stride=apart), :] = p_scr[slot].T
        return carry

    lax.fori_loop(0, views // slots, some_views, 0)
    chunk = 1024
    steps = views * width // chunk
    weight = w_ref[:, pl.ds(pl.multiple_of(jnp.where(first_core, 128, 0), 128), 256)]
    center = None
    total = squares = 0.0
    for i in range(steps):
        rows = slice(i * chunk, (i + 1) * chunk)
        columns = range(i * chunk // views, (i + 1) * chunk // views)
        patch = jnp.concatenate([t_scr[w * apart : w * apart + views, :] for w in columns], axis=0).astype(BF)
        pt_ref[rows, :] = patch
        raw = dot(patch, weight).reshape(chunk // views, views, 256)
        if center is None:
            start = jnp.sum(raw, axis=0)
            center = fold(start[:, :128] + start[:, 128:]) * (1.0 / (8 * chunk // views))
        for half in range(2):
            part = raw[:, :, half * 128 : half * 128 + 128] - center[None]
            total = total + jnp.sum(part, axis=0)
            squares = squares + jnp.sum(part * part, axis=0)
    offset = fold(total) * (1.0 / (8 * width))
    st_ref[0:views, :] = center + offset
    st_ref[views:, :] = fold(squares) - offset * offset * (8.0 * width)


def row_mask(first, lanes):
    row = lax.axis_index("rows") * 4 + first + (lax.broadcasted_iota(jnp.int32, (1, lanes), 1) >> 5)
    return jnp.where((row >= 0) & (row < lax.axis_size("rows") * 4), 1.0, 0.0).astype(F32)


def merge(one, two, views, cells):
    gap = one[:views] - two[:views]
    mean = (one[:views] + two[:views]) * 0.5
    return mean, one[views:] + two[views:] + gap * gap * (0.5 * cells)


def tiled_lanes(scr, ref):
    scr[...] = jnp.zeros_like(scr)
    scr[0:1, 0:32] = ref[...]
    return fold(scr[...])[0:1]


def main_kernel(
    shifts, pt_ref, st_ref, other_ref, gain_ref, bias_ref, w1_ref, w2_ref, w3_ref, ca_hbm, cb_hbm, out_ref,
    nb, mid, f_scr, s_low, s_high, q_low, q_high, v32, vb, hb, ca_ref, cb_ref, g_scr, sems,
):
    copies = [
        pltpu.make_async_copy(ca_hbm, ca_ref, sems.at[0]),
        pltpu.make_async_copy(cb_hbm, cb_ref, sems.at[1]),
    ]
    for copy in copies:
        copy.start()
    s_scr, q_scr = (s_low, s_high), (q_low, q_high)
    views = st_ref.shape[0] // 2
    total = pt_ref.shape[0]
    planes = out_ref.shape[0]
    width = out_ref.shape[3]
    cells = lax.axis_size("rows") * 4 * width
    mean, squares = merge(st_ref[...], other_ref[...], views, cells // 2)
    scale = tiled_lanes(g_scr, gain_ref) / jnp.sqrt(squares * (1.0 / cells) + 1e-05)
    shift = tiled_lanes(g_scr, bias_ref)
    edge = jnp.zeros((views, 384), BF)
    nb[0:views, :] = edge
    nb[views + total :, :] = edge
    for block in range(2):
        mid[block, 0:views, :] = edge[:, :256]
        mid[block, views + total :, :] = edge[:, :256]
    size = 1024
    cols = size // views
    steps = total // size
    masks = [row_mask(4 * group - 4, 128) for group in range(3)]

    def normalize(i, carry):
        rows = pl.ds(pl.multiple_of(i * size, size), size)
        out = pl.ds(pl.multiple_of(i * size + views, views), size)
        raw = dot(pt_ref[rows, :], w1_ref[...])
        for group in range(3):
            part = raw[:, group * 128 : group * 128 + 128].reshape(cols, views, 128)
            part = jnp.maximum((part - mean[None]) * scale[None] + shift[None], 0.0) * masks[group][None]
            nb[out, group * 128 : group * 128 + 128] = part.reshape(size, 128).astype(BF)
        return carry

    mid_masks = [row_mask(4 * block - 3, 256) for block in range(2)]

    def middle(i, carry):
        out = pl.ds(pl.multiple_of(i * size + views, views), size)
        for block in range(2):
            taps = [
                nb[pl.ds(pl.multiple_of(i * size + b * views, views), size), block * 128 : block * 128 + 256]
                for b in range(3)
            ]
            part = dot(jnp.concatenate(taps, axis=1), w2_ref[...])
            part = jnp.maximum(part, 0.0) * mid_masks[block]
            mid[block, out, :] = part.astype(BF)
        return carry

    last_masks = [row_mask(4 * block - 2, 128) for block in range(2)]
    couples = 32
    apart = views + 1

    def last(i, carry):
        for block in range(2):
            rows = pl.ds(i * couples * 2 * views, (couples + 1) * 2 * views)
            value = mid[block, rows, :].reshape(couples + 1, 2, views, 256)
            taps = [value[j // 2 : j // 2 + couples, j % 2].reshape(couples * views, 256) for j in range(4)]
            part = dot(jnp.concatenate(taps, axis=1), w3_ref[...])
            for q in range(2):
                half = (part[:, q * 128 : q * 128 + 128] * last_masks[block]).astype(BF).astype(F32)
                for m in range(couples):
                    start = (block * width + (i * couples + m) * 2 + q) * apart
                    f_scr[start : start + views, :] = half[m * views : (m + 1) * views]

    for ref in s_scr + q_scr:
        ref[...] = jnp.zeros_like(ref)

    def add_views(i):
        for v in range(views):
            step = shifts[v, 0] + 4
            for block in range(2):
                feats = f_scr[pl.ds((block * width + i * cols) * apart + v, cols, stride=apart), :]
                s_scr[block][step, REACH + i * cols : REACH + (i + 1) * cols, :] += feats
                q_scr[block][step, REACH + i * cols : REACH + (i + 1) * cols, :] += feats * feats

    for i in range(steps + 3):
        if i < steps:
            normalize(i, 0)
        if 0 <= i - 1 < steps:
            middle(i - 1, 0)
        if 0 <= i - 2 < steps:
            last(i - 2, 0)
        if 0 <= i - 3 < steps:
            add_views(i - 3)

    for pair in (0, planes // 2):
        hb[pair, pair * 2 // planes] = jnp.zeros_like(hb[0, 0])
    vb[0] = jnp.zeros_like(vb[0])
    vb[planes + 1] = jnp.zeros_like(vb[0])
    v32[...] = jnp.zeros_like(v32)

    part_size = 32

    def one_plane(k, carry):
        for block in range(2):
            for part in range(width // part_size):
                start = REACH + part * part_size
                summed = s_scr[block][4, start : start + part_size, :]
                squares = q_scr[block][4, start : start + part_size, :]
                for step in (-4, -3, -2, -1, 1, 2, 3, 4):
                    rows = pl.ds(start + step * (k + 1), part_size)
                    summed = summed + s_scr[block][step + 4, rows, :]
                    squares = squares + q_scr[block][step + 4, rows, :]
                average = summed * (1.0 / views)
                value = (squares * (1.0 / views) - average * average).astype(BF)
                v32[k % 4, 8 + part * part_size : 8 + part * part_size + part_size, block * 128 : block * 128 + 128] = (
                    value.astype(F32)
                )
        for tap in range(3):
            vb[k + 1, :, tap * 256 : tap * 256 + 256] = v32[k % 4, 7 + tap : 7 + tap + width, :].astype(BF)
        return carry

    mask = row_mask(-1, 256)
    group = 2

    def hidden(i, carry):
        k = i * group
        value = dot(jnp.concatenate([vb[pl.ds(k + d, group)].reshape(group * width, 768) for d in range(3)], axis=1), ca_ref[...].reshape(2304, 256))
        value = (jnp.maximum(value, 0.0) * mask).astype(BF).astype(F32)
        for t in range(group):
            v32[4 + 2 * (i % 2) + t, 8 : 8 + width, :] = value[t * width : (t + 1) * width]
            plane = k + t + 1
            for tap in range(3):
                hb[plane // 2, plane % 2, :, tap * 256 : tap * 256 + 256] = v32[4 + 2 * (i % 2) + t, 7 + tap : 7 + tap + width, :].astype(BF)
        return carry

    pairs = 3

    def final(i, carry):
        j = i * pairs
        taps = [hb[pl.ds(j + p // 2, pairs), p % 2].reshape(pairs * width, 768) for p in range(4)]
        value = dot(jnp.concatenate(taps, axis=1), cb_ref[...].reshape(3072, 256))
        for t in range(pairs):
            part = value[t * width : (t + 1) * width].T
            out_ref[pl.ds(2 * (j + t), 2)] = part.astype(BF).reshape(2, 4, 32, width)
        return carry

    for copy in copies:
        copy.wait()
    for k in range(4):
        one_plane(k, 0)
    for i in range(6):
        hidden(i, 0)
        if i < 4:
            one_plane(2 * i + 4, 0)
            one_plane(2 * i + 5, 0)
    final(0, 0)
    final(1, 0)


def one_hot(rows, lanes, same):
    row = lax.broadcasted_iota(jnp.int32, (rows, lanes), 0)
    lane = lax.broadcasted_iota(jnp.int32, (rows, lanes), 1)
    return jnp.where(same(row, lane), 1.0, 0.0)


def tiled_blocks(w_ref, index, eye):
    return [
        lax.dot_general(w_ref[index(a)], eye, (((0,), (0,)), ((), ())), preferred_element_type=F32) for a in range(3)
    ]


def banded(blocks, row_in, used):
    group = lax.broadcasted_iota(jnp.int32, blocks[0].shape, 1) >> 5
    value = jnp.zeros_like(blocks[0])
    for a in range(3):
        if 0 <= row_in - a < used:
            value = jnp.where(group == row_in - a, blocks[a], value)
    return value.astype(BF)


def color_weights_kernel(w_ref, w1_ref):
    eye = one_hot(32, 384, lambda row, lane: row == (lane & 31)).astype(BF)
    colors = dot(w_ref[...], eye).astype(BF)
    place = lax.broadcasted_iota(jnp.int32, (128, 1), 0)
    tap = (place >= 42).astype(jnp.int32) + (place >= 84).astype(jnp.int32)
    inner = place - 42 * tap
    row_in = (inner * 171) >> 9
    source = jnp.where(place < 126, 3 * tap + inner - 3 * row_in, -99)
    lane = lax.broadcasted_iota(jnp.int32, (1, 27), 1)
    row_out = lax.broadcasted_iota(jnp.int32, (1, 384), 1) >> 5
    value = jnp.zeros((128, 384), F32)
    for a in range(3):
        picked = dot(jnp.where(lane == source + 9 * a, 1.0, 0.0).astype(BF), colors)
        value = jnp.where(row_out == row_in - a, picked, value)
    w1_ref[...] = value.astype(BF)


def feature_weights_kernel(wmid_ref, wout_ref, w2_ref, w3_ref):
    eye = one_hot(32, 256, lambda row, lane: row == (lane & 31)).astype(BF)
    for b in range(3):
        blocks = tiled_blocks(wmid_ref, lambda a: 3 * a + b, eye)
        for row_in in range(8):
            start = b * 256 + row_in * 32
            w2_ref[start : start + 32, :] = banded(blocks, row_in, 6)
        blocks = tiled_blocks(wout_ref, lambda a: 3 * a + b, eye[:, :128])
        for row_in in range(8):
            value = banded(blocks, row_in, 4)
            for q in range(2):
                start = (b + q) * 256 + row_in * 32
                w3_ref[start : start + 32, q * 128 : q * 128 + 128] = value
    w3_ref[0:256, 128:256] = jnp.zeros((256, 128), BF)
    w3_ref[768:1024, 0:128] = jnp.zeros((256, 128), BF)


def hidden_weights_kernel(w_ref, ca_ref):
    eye = one_hot(32, 256, lambda row, lane: row == (lane & 31)).astype(BF)
    for plane in range(3):
        for e in range(3):
            blocks = tiled_blocks(w_ref, lambda a: 9 * plane + 3 * a + e, eye)
            for row_in in range(8):
                start = e * 256 + row_in * 32
                ca_ref[plane, start : start + 32, :] = banded(blocks, row_in, 6)


def final_weights_kernel(w_ref, cb_ref):
    eye = one_hot(32, 128, lambda row, lane: row == (lane & 31)).astype(BF)
    blank = jnp.zeros((768, 128), BF)
    cb_ref[0, :, 128:256] = blank
    cb_ref[3, :, 0:128] = blank
    for plane in range(3):
        for e in range(3):
            blocks = tiled_blocks(w_ref, lambda a: 9 * plane + 3 * a + e, eye)
            for row_in in range(8):
                start = e * 256 + row_in * 32
                value = banded(blocks, row_in, 4)
                cb_ref[plane, start : start + 32, 0:128] = value
                cb_ref[plane + 1, start : start + 32, 128:256] = value


def send(value, axis, even, odd):
    count = lax.axis_size(axis)
    pairs = []
    for i in range(count):
        to = i + (odd if i % 2 else even)
        if not 0 <= to < count:
            to = i ^ 1 if abs(even) == 2 else i
        pairs.append((i, to))
    return lax.ppermute(value, axis, pairs)


def swap(value, axis, bit):
    count = lax.axis_size(axis)
    return lax.ppermute(value, axis, [(i, i ^ bit) for i in range(count)])


def limit(mib):
    return pltpu.CompilerParams(vmem_limit_bytes=mib * 1024 * 1024)


def shards(
    images,
    shifts,
    in_weight,
    norm_gain,
    norm_bias,
    mid_weight,
    out_weight,
    cost_weight_a,
    cost_weight_b,
):
    views, rows, colors, width = images.shape
    planes = shifts.shape[1]
    chan = in_weight.shape[2]
    count = lax.axis_size("rows")
    index = lax.axis_index("rows")
    core = index % 2
    total = views * width


    def weights(kernel, shapes, *operands):
        shapes = tuple(jax.ShapeDtypeStruct(shape, BF) for shape in shapes)
        size = 2 * sum(shape.size for shape in shapes)
        return pl.pallas_call(
            kernel,
            name=kernel.__name__,
            out_shape=shapes,
            in_specs=[VMEM] * len(operands),
            out_specs=(VMEM,) * len(shapes),
            cost_estimate=pl.CostEstimate(flops=size, bytes_accessed=2 * size, transcendentals=0),
            compiler_params=limit(8),
        )(*operands)

    own = images.reshape(views, rows * colors, width)
    head, tail = own[:, :colors], own[:, (rows - 1) * colors :]
    pair = swap(own, "rows", 1)
    far = send(own, "rows", -1, 1)
    near = send(jnp.where(core == 0, tail, head), "rows", 2, -2)
    after = send(jnp.where(core == 0, head, tail), "rows", -2, 2)
    colors_in = in_weight.transpose(0, 1, 3, 2).reshape(9 * colors, chan)
    (w1,) = weights(color_weights_kernel, [(128, 384)], colors_in)

    patches, stats = pl.pallas_call(
        stats_kernel,
        name="stats",
        out_shape=(
            jax.ShapeDtypeStruct((total, 128), BF),
            jax.ShapeDtypeStruct((2 * views, 128), F32),
        ),
        in_specs=[VMEM] * 6,
        out_specs=(VMEM, VMEM),
        scratch_shapes=[
            pltpu.VMEM((8, 48, width), F32),
            pltpu.VMEM((8, 128, width), F32),
            pltpu.VMEM(((width + 1) * (views + 1), 128), F32),
        ],
        compiler_params=limit(12),
    )(own, pair, far, near, after, w1)
    jobs = [
        (feature_weights_kernel, [(768, 256), (1024, 256)], (mid_weight.reshape(9, chan, chan), out_weight.reshape(9, chan, chan))),
        (hidden_weights_kernel, [(3, 768, 256)], (cost_weight_a.reshape(27, chan, chan),)),
        (final_weights_kernel, [(4, 768, 256)], (cost_weight_b.reshape(27, chan, chan),)),
    ]
    made = []
    bit = 2
    while True:
        last = 2 * bit >= count
        other = swap(stats, "rows", bit)
        while jobs:
            kernel, shapes, operands = jobs.pop(0)
            if bit > 2:
                stats, operands = lax.optimization_barrier((stats, operands))
            new = weights(kernel, shapes, *operands)
            if not last:
                other, new = lax.optimization_barrier((other, new))
            made.extend(new)
            if not last:
                break
        if last:
            break
        stats = jnp.concatenate(merge(stats, other, views, rows * width * bit), axis=0)
        bit *= 2
    w2, w3, ca, cb = made

    return pl.pallas_call(
        main_kernel,
        name="main",
        out_shape=jax.ShapeDtypeStruct((planes, rows, chan, width), BF),
        in_specs=[SMEM] + [VMEM] * 8 + [pl.BlockSpec(memory_space=pl.ANY)] * 2,
        out_specs=VMEM,
        scratch_shapes=[
            pltpu.VMEM((total + 2 * views, 384), BF),
            pltpu.VMEM((2, total + 2 * views, 256), BF),
            pltpu.VMEM(((2 * width + 1) * (views + 1), 128), F32),
            *[pltpu.VMEM((9, width + 2 * REACH, 128), F32) for _ in range(4)],
            pltpu.VMEM((8, width + 16, 256), F32),
            pltpu.VMEM((planes + 2, width, 768), BF),
            pltpu.VMEM((planes // 2 + 1, 2, width, 768), BF),
            pltpu.VMEM((3, 768, 256), BF),
            pltpu.VMEM((4, 768, 256), BF),
            pltpu.VMEM((8, 128), F32),
            pltpu.SemaphoreType.DMA((2,)),
        ],
        compiler_params=limit(44),
    )(shifts, patches, stats, other, norm_gain[None], norm_bias[None], w1, w2, w3, ca, cb)


def solution(mesh):
    placed = (P("groups", "rows", None, None), P("groups", None), P(), P(), P(), P(), P(), P(), P())
    return jax.shard_map(
        shards,
        mesh=mesh,
        in_specs=placed,
        out_specs=P("groups", "rows", None, None),
        check_vma=False,
    )
```

```python
import functools
import jax
import jax.numpy as jnp
from jax import lax
from jax.experimental import pallas as pl
from jax.experimental.pallas import tpu as pltpu
from jax.sharding import PartitionSpec as P

BF = jnp.bfloat16
F32 = jnp.float32
VMEM = pl.BlockSpec(memory_space=pltpu.VMEM)
SMEM = pl.BlockSpec(memory_space=pltpu.SMEM)
REACH = 48


def dot(a, b):
    return jnp.dot(a, b, preferred_element_type=F32)


def fold(sums):
    sums = sums + pltpu.roll(sums, 64, 1)
    return sums + pltpu.roll(sums, 32, 1)


def stats_kernel(own_ref, pair_ref, far_ref, near_ref, next_ref, w_ref, pt_ref, st_ref, x_scr, p_scr, t_scr):
    views, tall, width = own_ref.shape
    index = lax.axis_index("rows")
    first_core = index % 2 == 0
    top = (index >= 2).astype(F32)
    bottom = (index < lax.axis_size("rows") - 2).astype(F32)
    beyond = jnp.where(first_core, top, bottom)
    lane = lax.broadcasted_iota(jnp.int32, (1, width), 1)
    p_scr[...] = jnp.zeros_like(p_scr)
    slots = p_scr.shape[0]
    apart = views + 1

    def some_views(i, carry):
        for slot in range(slots):
            v = i * slots + slot
            pair = pair_ref[v].astype(F32)
            far = far_ref[v].astype(F32) * beyond
            one = near_ref[v].astype(F32)
            two = next_ref[v].astype(F32)
            x_scr[slot, 0:3, :] = jnp.where(first_core, one, two) * top
            x_scr[slot, 3:15, :] = jnp.where(first_core, far, pair)
            x_scr[slot, 15:27, :] = own_ref[v].astype(F32)
            x_scr[slot, 27:39, :] = jnp.where(first_core, pair, far)
            x_scr[slot, 39:42, :] = jnp.where(first_core, two, one) * bottom
            x = x_scr[slot, 0:42, :]
            p_scr[slot, 0:42, :] = jnp.where(lane == 0, 0.0, pltpu.roll(x, 1, 1))
            p_scr[slot, 42:84, :] = x
            p_scr[slot, 84:126, :] = jnp.where(lane == width - 1, 0.0, pltpu.roll(x, width - 1, 1))
            t_scr[pl.ds(v, width, stride=apart), :] = p_scr[slot].T
        return carry

    lax.fori_loop(0, views // slots, some_views, 0)
    chunk = 1024
    steps = views * width // chunk
    weight = w_ref[:, pl.ds(pl.multiple_of(jnp.where(first_core, 128, 0), 128), 256)]
    center = None
    total = squares = 0.0
    for i in range(steps):
        rows = slice(i * chunk, (i + 1) * chunk)
        columns = range(i * chunk // views, (i + 1) * chunk // views)
        patch = jnp.concatenate([t_scr[w * apart : w * apart + views, :] for w in columns], axis=0).astype(BF)
        pt_ref[rows, :] = patch
        raw = dot(patch, weight).reshape(chunk // views, views, 256)
        if center is None:
            start = jnp.sum(raw, axis=0)
            center = fold(start[:, :128] + start[:, 128:]) * (1.0 / (8 * chunk // views))
        for half in range(2):
            part = raw[:, :, half * 128 : half * 128 + 128] - center[None]
            total = total + jnp.sum(part, axis=0)
            squares = squares + jnp.sum(part * part, axis=0)
    offset = fold(total) * (1.0 / (8 * width))
    st_ref[0:views, :] = center + offset
    st_ref[views:, :] = fold(squares) - offset * offset * (8.0 * width)


def raw_kernel(start, pt_ref, w1_ref, raw_ref):
    for i in range(raw_ref.shape[0] // 1024):
        rows = slice(i * 1024, (i + 1) * 1024)
        raw_ref[rows, :] = dot(pt_ref[start + i * 1024 : start + (i + 1) * 1024, :], w1_ref[...])


def row_mask(first, lanes):
    row = lax.axis_index("rows") * 4 + first + (lax.broadcasted_iota(jnp.int32, (1, lanes), 1) >> 5)
    return jnp.where((row >= 0) & (row < lax.axis_size("rows") * 4), 1.0, 0.0).astype(F32)


def merge(one, two, views, cells):
    gap = one[:views] - two[:views]
    mean = (one[:views] + two[:views]) * 0.5
    return mean, one[views:] + two[views:] + gap * gap * (0.5 * cells)


def tiled_lanes(scr, ref):
    scr[...] = jnp.zeros_like(scr)
    scr[0:1, 0:32] = ref[...]
    return fold(scr[...])[0:1]


def main_kernel(
    shifts, low_ref, high_ref, st_ref, other_ref, gain_ref, bias_ref, w2_ref, w3_ref, ca_hbm, cb_hbm, out_ref,
    nb, mid, f_scr, s_low, s_high, q_low, q_high, v32, vb, hb, ca_ref, cb_ref, g_scr, sems,
):
    copies = [
        pltpu.make_async_copy(ca_hbm, ca_ref, sems.at[0]),
        pltpu.make_async_copy(cb_hbm, cb_ref, sems.at[1]),
    ]
    for copy in copies:
        copy.start()
    s_scr, q_scr = (s_low, s_high), (q_low, q_high)
    views = st_ref.shape[0] // 2
    total = 2 * low_ref.shape[0]
    planes = out_ref.shape[0]
    width = out_ref.shape[3]
    cells = lax.axis_size("rows") * 4 * width
    mean, squares = merge(st_ref[...], other_ref[...], views, cells // 2)
    scale = tiled_lanes(g_scr, gain_ref) / jnp.sqrt(squares * (1.0 / cells) + 1e-05)
    shift = tiled_lanes(g_scr, bias_ref)
    edge = jnp.zeros((views, 384), BF)
    nb[0:views, :] = edge
    nb[views + total :, :] = edge
    for block in range(2):
        mid[block, 0:views, :] = edge[:, :256]
        mid[block, views + total :, :] = edge[:, :256]
    size = 1024
    cols = size // views
    steps = total // size
    masks = [row_mask(4 * group - 4, 128) for group in range(3)]

    def normalize(i, carry):
        out = pl.ds(pl.multiple_of(i * size + views, views), size)
        half = steps // 2
        raw_ref = low_ref if i < half else high_ref
        raw = raw_ref[i % half * size : (i % half + 1) * size, :]
        for group in range(3):
            part = raw[:, group * 128 : group * 128 + 128].reshape(cols, views, 128)
            part = jnp.maximum((part - mean[None]) * scale[None] + shift[None], 0.0) * masks[group][None]
            nb[out, group * 128 : group * 128 + 128] = part.reshape(size, 128).astype(BF)
        return carry

    mid_masks = [row_mask(4 * block - 3, 256) for block in range(2)]

    def middle(i, carry):
        out = pl.ds(pl.multiple_of(i * size + views, views), size)
        for block in range(2):
            taps = [
                nb[pl.ds(pl.multiple_of(i * size + b * views, views), size), block * 128 : block * 128 + 256]
                for b in range(3)
            ]
            part = dot(jnp.concatenate(taps, axis=1), w2_ref[...])
            part = jnp.maximum(part, 0.0) * mid_masks[block]
            mid[block, out, :] = part.astype(BF)
        return carry

    last_masks = [row_mask(4 * block - 2, 128) for block in range(2)]
    couples = 32
    apart = views + 1

    def last(i, carry):
        for block in range(2):
            rows = pl.ds(i * couples * 2 * views, (couples + 1) * 2 * views)
            value = mid[block, rows, :].reshape(couples + 1, 2, views, 256)
            taps = [value[j // 2 : j // 2 + couples, j % 2].reshape(couples * views, 256) for j in range(4)]
            part = dot(jnp.concatenate(taps, axis=1), w3_ref[...])
            for q in range(2):
                half = (part[:, q * 128 : q * 128 + 128] * last_masks[block]).astype(BF).astype(F32)
                for m in range(couples):
                    start = (block * width + (i * couples + m) * 2 + q) * apart
                    f_scr[start : start + views, :] = half[m * views : (m + 1) * views]

    for ref in s_scr + q_scr:
        ref[...] = jnp.zeros_like(ref)

    def add_views(i):
        for v in range(views):
            step = shifts[v, 0] + 4
            for block in range(2):
                feats = f_scr[pl.ds((block * width + i * cols) * apart + v, cols, stride=apart), :]
                s_scr[block][step, REACH + i * cols : REACH + (i + 1) * cols, :] += feats
                q_scr[block][step, REACH + i * cols : REACH + (i + 1) * cols, :] += feats * feats

    for i in range(steps + 3):
        if i < steps:
            normalize(i, 0)
        if 0 <= i - 1 < steps:
            middle(i - 1, 0)
        if 0 <= i - 2 < steps:
            last(i - 2, 0)
        if 0 <= i - 3 < steps:
            add_views(i - 3)

    for pair in (0, planes // 2):
        hb[pair, pair * 2 // planes] = jnp.zeros_like(hb[0, 0])
    vb[0] = jnp.zeros_like(vb[0])
    vb[planes + 1] = jnp.zeros_like(vb[0])
    v32[...] = jnp.zeros_like(v32)

    part_size = 32

    def one_plane(k, carry):
        for block in range(2):
            for part in range(width // part_size):
                start = REACH + part * part_size
                summed = s_scr[block][4, start : start + part_size, :]
                squares = q_scr[block][4, start : start + part_size, :]
                for step in (-4, -3, -2, -1, 1, 2, 3, 4):
                    rows = pl.ds(start + step * (k + 1), part_size)
                    summed = summed + s_scr[block][step + 4, rows, :]
                    squares = squares + q_scr[block][step + 4, rows, :]
                average = summed * (1.0 / views)
                value = (squares * (1.0 / views) - average * average).astype(BF)
                v32[k % 4, 8 + part * part_size : 8 + part * part_size + part_size, block * 128 : block * 128 + 128] = (
                    value.astype(F32)
                )
        for tap in range(3):
            vb[k + 1, :, tap * 256 : tap * 256 + 256] = v32[k % 4, 7 + tap : 7 + tap + width, :].astype(BF)
        return carry

    mask = row_mask(-1, 256)
    group = 2

    def hidden(i, carry):
        k = i * group
        value = dot(jnp.concatenate([vb[pl.ds(k + d, group)].reshape(group * width, 768) for d in range(3)], axis=1), ca_ref[...].reshape(2304, 256))
        value = (jnp.maximum(value, 0.0) * mask).astype(BF).astype(F32)
        for t in range(group):
            v32[4 + 2 * (i % 2) + t, 8 : 8 + width, :] = value[t * width : (t + 1) * width]
            plane = k + t + 1
            for tap in range(3):
                hb[plane // 2, plane % 2, :, tap * 256 : tap * 256 + 256] = v32[4 + 2 * (i % 2) + t, 7 + tap : 7 + tap + width, :].astype(BF)
        return carry

    pairs = 3

    def final(i, carry):
        j = i * pairs
        taps = [hb[pl.ds(j + p // 2, pairs), p % 2].reshape(pairs * width, 768) for p in range(4)]
        value = dot(jnp.concatenate(taps, axis=1), cb_ref[...].reshape(3072, 256))
        for t in range(pairs):
            part = value[t * width : (t + 1) * width].T
            out_ref[pl.ds(2 * (j + t), 2)] = part.astype(BF).reshape(2, 4, 32, width)
        return carry

    for copy in copies:
        copy.wait()
    for k in range(4):
        one_plane(k, 0)
    for i in range(6):
        hidden(i, 0)
        if i < 4:
            one_plane(2 * i + 4, 0)
            one_plane(2 * i + 5, 0)
    final(0, 0)
    final(1, 0)


def one_hot(rows, lanes, same):
    row = lax.broadcasted_iota(jnp.int32, (rows, lanes), 0)
    lane = lax.broadcasted_iota(jnp.int32, (rows, lanes), 1)
    return jnp.where(same(row, lane), 1.0, 0.0)


def tiled_blocks(w_ref, index, eye):
    return [
        lax.dot_general(w_ref[index(a)], eye, (((0,), (0,)), ((), ())), preferred_element_type=F32) for a in range(3)
    ]


def banded(blocks, row_in, used):
    group = lax.broadcasted_iota(jnp.int32, blocks[0].shape, 1) >> 5
    value = jnp.zeros_like(blocks[0])
    for a in range(3):
        if 0 <= row_in - a < used:
            value = jnp.where(group == row_in - a, blocks[a], value)
    return value.astype(BF)


def color_weights_kernel(w_ref, w1_ref):
    eye = one_hot(32, 384, lambda row, lane: row == (lane & 31)).astype(BF)
    colors = dot(w_ref[...], eye).astype(BF)
    place = lax.broadcasted_iota(jnp.int32, (128, 1), 0)
    tap = (place >= 42).astype(jnp.int32) + (place >= 84).astype(jnp.int32)
    inner = place - 42 * tap
    row_in = (inner * 171) >> 9
    source = jnp.where(place < 126, 3 * tap + inner - 3 * row_in, -99)
    lane = lax.broadcasted_iota(jnp.int32, (1, 27), 1)
    row_out = lax.broadcasted_iota(jnp.int32, (1, 384), 1) >> 5
    value = jnp.zeros((128, 384), F32)
    for a in range(3):
        picked = dot(jnp.where(lane == source + 9 * a, 1.0, 0.0).astype(BF), colors)
        value = jnp.where(row_out == row_in - a, picked, value)
    w1_ref[...] = value.astype(BF)


def feature_weights_kernel(wmid_ref, wout_ref, w2_ref, w3_ref):
    eye = one_hot(32, 256, lambda row, lane: row == (lane & 31)).astype(BF)
    for b in range(3):
        blocks = tiled_blocks(wmid_ref, lambda a: 3 * a + b, eye)
        for row_in in range(8):
            start = b * 256 + row_in * 32
            w2_ref[start : start + 32, :] = banded(blocks, row_in, 6)
        blocks = tiled_blocks(wout_ref, lambda a: 3 * a + b, eye[:, :128])
        for row_in in range(8):
            value = banded(blocks, row_in, 4)
            for q in range(2):
                start = (b + q) * 256 + row_in * 32
                w3_ref[start : start + 32, q * 128 : q * 128 + 128] = value
    w3_ref[0:256, 128:256] = jnp.zeros((256, 128), BF)
    w3_ref[768:1024, 0:128] = jnp.zeros((256, 128), BF)


def hidden_weights_kernel(w_ref, ca_ref):
    eye = one_hot(32, 256, lambda row, lane: row == (lane & 31)).astype(BF)
    for plane in range(3):
        for e in range(3):
            blocks = tiled_blocks(w_ref, lambda a: 9 * plane + 3 * a + e, eye)
            for row_in in range(8):
                start = e * 256 + row_in * 32
                ca_ref[plane, start : start + 32, :] = banded(blocks, row_in, 6)


def final_weights_kernel(w_ref, cb_ref):
    eye = one_hot(32, 128, lambda row, lane: row == (lane & 31)).astype(BF)
    blank = jnp.zeros((768, 128), BF)
    cb_ref[0, :, 128:256] = blank
    cb_ref[3, :, 0:128] = blank
    for plane in range(3):
        for e in range(3):
            blocks = tiled_blocks(w_ref, lambda a: 9 * plane + 3 * a + e, eye)
            for row_in in range(8):
                start = e * 256 + row_in * 32
                value = banded(blocks, row_in, 4)
                cb_ref[plane, start : start + 32, 0:128] = value
                cb_ref[plane + 1, start : start + 32, 128:256] = value


def send(value, axis, even, odd):
    count = lax.axis_size(axis)
    pairs = []
    for i in range(count):
        to = i + (odd if i % 2 else even)
        if not 0 <= to < count:
            to = i ^ 1 if abs(even) == 2 else i
        pairs.append((i, to))
    return lax.ppermute(value, axis, pairs)


def swap(value, axis, bit):
    count = lax.axis_size(axis)
    return lax.ppermute(value, axis, [(i, i ^ bit) for i in range(count)])


def limit(mib):
    return pltpu.CompilerParams(vmem_limit_bytes=mib * 1024 * 1024)


def shards(
    images,
    shifts,
    in_weight,
    norm_gain,
    norm_bias,
    mid_weight,
    out_weight,
    cost_weight_a,
    cost_weight_b,
):
    views, rows, colors, width = images.shape
    planes = shifts.shape[1]
    chan = in_weight.shape[2]
    count = lax.axis_size("rows")
    index = lax.axis_index("rows")
    core = index % 2
    total = views * width


    def weights(kernel, shapes, *operands):
        shapes = tuple(jax.ShapeDtypeStruct(shape, BF) for shape in shapes)
        size = 2 * sum(shape.size for shape in shapes)
        return pl.pallas_call(
            kernel,
            name=kernel.__name__,
            out_shape=shapes,
            in_specs=[VMEM] * len(operands),
            out_specs=(VMEM,) * len(shapes),
            cost_estimate=pl.CostEstimate(flops=size, bytes_accessed=2 * size, transcendentals=0),
            compiler_params=limit(8),
        )(*operands)

    own = images.reshape(views, rows * colors, width)
    head, tail = own[:, :colors], own[:, (rows - 1) * colors :]
    pair = swap(own, "rows", 1)
    far = send(own, "rows", -1, 1)
    near = send(jnp.where(core == 0, tail, head), "rows", 2, -2)
    after = send(jnp.where(core == 0, head, tail), "rows", -2, 2)
    colors_in = in_weight.transpose(0, 1, 3, 2).reshape(9 * colors, chan)
    (w1,) = weights(color_weights_kernel, [(128, 384)], colors_in)

    patches, stats = pl.pallas_call(
        stats_kernel,
        name="stats",
        out_shape=(
            jax.ShapeDtypeStruct((total, 128), BF),
            jax.ShapeDtypeStruct((2 * views, 128), F32),
        ),
        in_specs=[VMEM] * 6,
        out_specs=(VMEM, VMEM),
        scratch_shapes=[
            pltpu.VMEM((8, 48, width), F32),
            pltpu.VMEM((8, 128, width), F32),
            pltpu.VMEM(((width + 1) * (views + 1), 128), F32),
        ],
        compiler_params=limit(12),
    )(own, pair, far, near, after, w1)
    jobs = [
        (feature_weights_kernel, [(768, 256), (1024, 256)], (mid_weight.reshape(9, chan, chan), out_weight.reshape(9, chan, chan))),
        (hidden_weights_kernel, [(3, 768, 256)], (cost_weight_a.reshape(27, chan, chan),)),
        (final_weights_kernel, [(4, 768, 256)], (cost_weight_b.reshape(27, chan, chan),)),
    ]
    made, raw = [], []
    bit = 2
    while True:
        last = 2 * bit >= count
        other = swap(stats, "rows", bit)
        last = 2 * bit >= count
        if last or 4 * bit >= count:
            stats, source = lax.optimization_barrier((stats, patches))
            half = pl.pallas_call(
                functools.partial(raw_kernel, len(raw) * (total // 2)),
                name="raw",
                out_shape=jax.ShapeDtypeStruct((total // 2, 384), F32),
                in_specs=[VMEM] * 2,
                out_specs=VMEM,
                cost_estimate=pl.CostEstimate(flops=total * 128 * 384, bytes_accessed=4000000, transcendentals=0),
                compiler_params=limit(8),
            )(source, w1)
            if not last:
                other, half = lax.optimization_barrier((other, half))
            raw.append(half)
        while jobs:
            kernel, shapes, operands = jobs.pop(0)
            if bit > 2:
                stats, operands = lax.optimization_barrier((stats, operands))
            new = weights(kernel, shapes, *operands)
            if not last:
                other, new = lax.optimization_barrier((other, new))
            made.extend(new)
            if not last:
                break
        if last:
            break
        stats = jnp.concatenate(merge(stats, other, views, rows * width * bit), axis=0)
        bit *= 2
    w2, w3, ca, cb = made

    return pl.pallas_call(
        main_kernel,
        name="main",
        out_shape=jax.ShapeDtypeStruct((planes, rows, chan, width), BF),
        in_specs=[SMEM] + [VMEM] * 8 + [pl.BlockSpec(memory_space=pl.ANY)] * 2,
        out_specs=VMEM,
        scratch_shapes=[
            pltpu.VMEM((total + 2 * views, 384), BF),
            pltpu.VMEM((2, total + 2 * views, 256), BF),
            pltpu.VMEM(((2 * width + 1) * (views + 1), 128), F32),
            *[pltpu.VMEM((9, width + 2 * REACH, 128), F32) for _ in range(4)],
            pltpu.VMEM((8, width + 16, 256), F32),
            pltpu.VMEM((planes + 2, width, 768), BF),
            pltpu.VMEM((planes // 2 + 1, 2, width, 768), BF),
            pltpu.VMEM((3, 768, 256), BF),
            pltpu.VMEM((4, 768, 256), BF),
            pltpu.VMEM((8, 128), F32),
            pltpu.SemaphoreType.DMA((2,)),
        ],
        compiler_params=limit(40),
    )(shifts, *raw, stats, other, norm_gain[None], norm_bias[None], w2, w3, ca, cb)


def solution(mesh):
    placed = (P("groups", "rows", None, None), P("groups", None), P(), P(), P(), P(), P(), P(), P())
    return jax.shard_map(
        shards,
        mesh=mesh,
        in_specs=placed,
        out_specs=P("groups", "rows", None, None),
        check_vma=False,
    )
```

```python
import functools
import jax
import jax.numpy as jnp
from jax import lax
from jax.experimental import pallas as pl
from jax.experimental.pallas import tpu as pltpu
from jax.sharding import PartitionSpec as P

BF = jnp.bfloat16
F32 = jnp.float32
VMEM = pl.BlockSpec(memory_space=pltpu.VMEM)
SMEM = pl.BlockSpec(memory_space=pltpu.SMEM)
REACH = 48


def dot(a, b):
    return jnp.dot(a, b, preferred_element_type=F32)


def fold(sums):
    sums = sums + pltpu.roll(sums, 64, 1)
    return sums + pltpu.roll(sums, 32, 1)


def stats_kernel(own_ref, pair_ref, far_ref, near_ref, next_ref, w_ref, pt_ref, st_ref, x_scr, p_scr, t_scr):
    views, tall, width = own_ref.shape
    index = lax.axis_index("rows")
    first_core = index % 2 == 0
    top = (index >= 2).astype(F32)
    bottom = (index < lax.axis_size("rows") - 2).astype(F32)
    beyond = jnp.where(first_core, top, bottom)
    lane = lax.broadcasted_iota(jnp.int32, (1, width), 1)
    p_scr[...] = jnp.zeros_like(p_scr)
    slots = p_scr.shape[0]
    apart = views + 1

    def some_views(i, carry):
        for slot in range(slots):
            v = i * slots + slot
            pair = pair_ref[v].astype(F32)
            far = far_ref[v].astype(F32) * beyond
            one = near_ref[v].astype(F32)
            two = next_ref[v].astype(F32)
            x_scr[slot, 0:3, :] = jnp.where(first_core, one, two) * top
            x_scr[slot, 3:15, :] = jnp.where(first_core, far, pair)
            x_scr[slot, 15:27, :] = own_ref[v].astype(F32)
            x_scr[slot, 27:39, :] = jnp.where(first_core, pair, far)
            x_scr[slot, 39:42, :] = jnp.where(first_core, two, one) * bottom
            x = x_scr[slot, 0:42, :]
            p_scr[slot, 0:42, :] = jnp.where(lane == 0, 0.0, pltpu.roll(x, 1, 1))
            p_scr[slot, 42:84, :] = x
            p_scr[slot, 84:126, :] = jnp.where(lane == width - 1, 0.0, pltpu.roll(x, width - 1, 1))
            t_scr[pl.ds(v, width, stride=apart), :] = p_scr[slot].T
        return carry

    lax.fori_loop(0, views // slots, some_views, 0)
    chunk = 1024
    steps = views * width // chunk
    weight = w_ref[:, pl.ds(pl.multiple_of(jnp.where(first_core, 128, 0), 128), 256)]
    center = None
    total = squares = 0.0
    for i in range(steps):
        rows = slice(i * chunk, (i + 1) * chunk)
        columns = range(i * chunk // views, (i + 1) * chunk // views)
        patch = jnp.concatenate([t_scr[w * apart : w * apart + views, :] for w in columns], axis=0).astype(BF)
        pt_ref[rows, :] = patch
        raw = dot(patch, weight).reshape(chunk // views, views, 256)
        if center is None:
            start = jnp.sum(raw, axis=0)
            center = fold(start[:, :128] + start[:, 128:]) * (1.0 / (8 * chunk // views))
        for half in range(2):
            part = raw[:, :, half * 128 : half * 128 + 128] - center[None]
            total = total + jnp.sum(part, axis=0)
            squares = squares + jnp.sum(part * part, axis=0)
    offset = fold(total) * (1.0 / (8 * width))
    st_ref[0:views, :] = center + offset
    st_ref[views:, :] = fold(squares) - offset * offset * (8.0 * width)


def raw_kernel(start, pt_ref, w1_ref, raw_ref):
    for i in range(raw_ref.shape[0] // 1024):
        rows = slice(i * 1024, (i + 1) * 1024)
        raw_ref[rows, :] = dot(pt_ref[start + i * 1024 : start + (i + 1) * 1024, :], w1_ref[...])


def row_mask(first, lanes):
    row = lax.axis_index("rows") * 4 + first + (lax.broadcasted_iota(jnp.int32, (1, lanes), 1) >> 5)
    return jnp.where((row >= 0) & (row < lax.axis_size("rows") * 4), 1.0, 0.0).astype(F32)


def merge(one, two, views, cells):
    gap = one[:views] - two[:views]
    mean = (one[:views] + two[:views]) * 0.5
    return mean, one[views:] + two[views:] + gap * gap * (0.5 * cells)


def tiled_lanes(scr, ref):
    scr[...] = jnp.zeros_like(scr)
    scr[0:1, 0:32] = ref[...]
    return fold(scr[...])[0:1]


def main_kernel(
    shifts, low_ref, high_ref, st_ref, other_ref, gain_ref, bias_ref, w2_ref, w3_ref, ca_hbm, cb_hbm, out_ref,
    nb, mid, f_scr, s_low, s_high, q_low, q_high, v32, vb, hb, ca_ref, cb_ref, g_scr, sems,
):
    copies = [
        pltpu.make_async_copy(ca_hbm, ca_ref, sems.at[0]),
        pltpu.make_async_copy(cb_hbm, cb_ref, sems.at[1]),
    ]
    for copy in copies:
        copy.start()
    s_scr, q_scr = (s_low, s_high), (q_low, q_high)
    views = st_ref.shape[0] // 2
    total = 2 * low_ref.shape[0]
    planes = out_ref.shape[0]
    width = out_ref.shape[3]
    cells = lax.axis_size("rows") * 4 * width
    mean, squares = merge(st_ref[...], other_ref[...], views, cells // 2)
    scale = tiled_lanes(g_scr, gain_ref) / jnp.sqrt(squares * (1.0 / cells) + 1e-05)
    shift = tiled_lanes(g_scr, bias_ref)
    edge = jnp.zeros((views, 384), BF)
    nb[0:views, :] = edge
    nb[views + total :, :] = edge
    for block in range(2):
        mid[block, 0:views, :] = edge[:, :256]
        mid[block, views + total :, :] = edge[:, :256]
    size = 1024
    cols = size // views
    steps = total // size
    masks = [row_mask(4 * group - 4, 128) for group in range(3)]

    def normalize(i, carry):
        out = pl.ds(pl.multiple_of(i * size + views, views), size)
        half = steps // 2
        raw_ref = low_ref if i < half else high_ref
        raw = raw_ref[i % half * size : (i % half + 1) * size, :]
        for group in range(3):
            part = raw[:, group * 128 : group * 128 + 128].reshape(cols, views, 128)
            part = jnp.maximum((part - mean[None]) * scale[None] + shift[None], 0.0) * masks[group][None]
            nb[out, group * 128 : group * 128 + 128] = part.reshape(size, 128).astype(BF)
        return carry

    mid_masks = [row_mask(4 * block - 3, 256) for block in range(2)]

    def middle(i, carry):
        out = pl.ds(pl.multiple_of(i * size + views, views), size)
        for block in range(2):
            taps = [
                nb[pl.ds(pl.multiple_of(i * size + b * views, views), size), block * 128 : block * 128 + 256]
                for b in range(3)
            ]
            part = dot(jnp.concatenate(taps, axis=1), w2_ref[...])
            part = jnp.maximum(part, 0.0) * mid_masks[block]
            mid[block, out, :] = part.astype(BF)
        return carry

    last_masks = [row_mask(4 * block - 2, 128) for block in range(2)]
    couples = 32
    apart = views + 1

    def last(i, carry):
        for block in range(2):
            rows = pl.ds(i * couples * 2 * views, (couples + 1) * 2 * views)
            value = mid[block, rows, :].reshape(couples + 1, 2, views, 256)
            taps = [value[j // 2 : j // 2 + couples, j % 2].reshape(couples * views, 256) for j in range(4)]
            part = dot(jnp.concatenate(taps, axis=1), w3_ref[...])
            for q in range(2):
                half = (part[:, q * 128 : q * 128 + 128] * last_masks[block]).astype(BF).astype(F32)
                for m in range(couples):
                    start = (block * width + (i * couples + m) * 2 + q) * apart
                    f_scr[start : start + views, :] = half[m * views : (m + 1) * views]

    for ref in s_scr + q_scr:
        ref[...] = jnp.zeros_like(ref)

    def add_views(i):
        for v in range(views):
            step = shifts[v, 0] + 4
            for block in range(2):
                feats = f_scr[pl.ds((block * width + i * cols) * apart + v, cols, stride=apart), :]
                s_scr[block][step, REACH + i * cols : REACH + (i + 1) * cols, :] += feats
                q_scr[block][step, REACH + i * cols : REACH + (i + 1) * cols, :] += feats * feats

    for i in range(steps + 3):
        if i < steps:
            normalize(i, 0)
        if 0 <= i - 1 < steps:
            middle(i - 1, 0)
        if 0 <= i - 2 < steps:
            last(i - 2, 0)
        if 0 <= i - 3 < steps:
            add_views(i - 3)

    for pair in (0, planes // 2):
        hb[pair, pair * 2 // planes] = jnp.zeros_like(hb[0, 0])
    vb[0] = jnp.zeros_like(vb[0])
    vb[planes + 1] = jnp.zeros_like(vb[0])
    v32[...] = jnp.zeros_like(v32)

    part_size = 32

    def one_plane(k, carry):
        for block in range(2):
            for part in range(width // part_size):
                start = REACH + part * part_size
                summed = s_scr[block][4, start : start + part_size, :]
                squares = q_scr[block][4, start : start + part_size, :]
                for step in (-4, -3, -2, -1, 1, 2, 3, 4):
                    rows = pl.ds(start + step * (k + 1), part_size)
                    summed = summed + s_scr[block][step + 4, rows, :]
                    squares = squares + q_scr[block][step + 4, rows, :]
                average = summed * (1.0 / views)
                value = (squares * (1.0 / views) - average * average).astype(BF)
                v32[k % 4, 8 + part * part_size : 8 + part * part_size + part_size, block * 128 : block * 128 + 128] = (
                    value.astype(F32)
                )
        for tap in range(3):
            vb[k + 1, :, tap * 256 : tap * 256 + 256] = v32[k % 4, 7 + tap : 7 + tap + width, :].astype(BF)
        return carry

    mask = row_mask(-1, 256)
    group = 2

    def hidden(i, carry):
        k = i * group
        value = dot(jnp.concatenate([vb[pl.ds(k + d, group)].reshape(group * width, 768) for d in range(3)], axis=1), ca_ref[...].reshape(2304, 256))
        value = (jnp.maximum(value, 0.0) * mask).astype(BF).astype(F32)
        for t in range(group):
            v32[4 + 2 * (i % 2) + t, 8 : 8 + width, :] = value[t * width : (t + 1) * width]
            plane = k + t + 1
            for tap in range(3):
                hb[plane // 2, plane % 2, :, tap * 256 : tap * 256 + 256] = v32[4 + 2 * (i % 2) + t, 7 + tap : 7 + tap + width, :].astype(BF)
        return carry

    pairs = 3

    def final(i, carry):
        j = i * pairs
        taps = [hb[pl.ds(j + p // 2, pairs), p % 2].reshape(pairs * width, 768) for p in range(4)]
        value = dot(jnp.concatenate(taps, axis=1), cb_ref[...].reshape(3072, 256))
        for t in range(pairs):
            part = value[t * width : (t + 1) * width].T
            out_ref[pl.ds(2 * (j + t), 2)] = part.astype(BF).reshape(2, 4, 32, width)
        return carry

    for copy in copies:
        copy.wait()
    for k in range(4):
        one_plane(k, 0)
    for i in range(6):
        hidden(i, 0)
        if i < 4:
            one_plane(2 * i + 4, 0)
            one_plane(2 * i + 5, 0)
        if i == 3:
            final(0, 0)
    final(1, 0)


def one_hot(rows, lanes, same):
    row = lax.broadcasted_iota(jnp.int32, (rows, lanes), 0)
    lane = lax.broadcasted_iota(jnp.int32, (rows, lanes), 1)
    return jnp.where(same(row, lane), 1.0, 0.0)


def tiled_blocks(w_ref, index, eye):
    return [
        lax.dot_general(w_ref[index(a)], eye, (((0,), (0,)), ((), ())), preferred_element_type=F32) for a in range(3)
    ]


def banded(blocks, row_in, used):
    group = lax.broadcasted_iota(jnp.int32, blocks[0].shape, 1) >> 5
    value = jnp.zeros_like(blocks[0])
    for a in range(3):
        if 0 <= row_in - a < used:
            value = jnp.where(group == row_in - a, blocks[a], value)
    return value.astype(BF)


def color_weights_kernel(w_ref, w1_ref):
    eye = one_hot(32, 384, lambda row, lane: row == (lane & 31)).astype(BF)
    colors = dot(w_ref[...], eye).astype(BF)
    place = lax.broadcasted_iota(jnp.int32, (128, 1), 0)
    tap = (place >= 42).astype(jnp.int32) + (place >= 84).astype(jnp.int32)
    inner = place - 42 * tap
    row_in = (inner * 171) >> 9
    source = jnp.where(place < 126, 3 * tap + inner - 3 * row_in, -99)
    lane = lax.broadcasted_iota(jnp.int32, (1, 27), 1)
    row_out = lax.broadcasted_iota(jnp.int32, (1, 384), 1) >> 5
    value = jnp.zeros((128, 384), F32)
    for a in range(3):
        picked = dot(jnp.where(lane == source + 9 * a, 1.0, 0.0).astype(BF), colors)
        value = jnp.where(row_out == row_in - a, picked, value)
    w1_ref[...] = value.astype(BF)


def feature_weights_kernel(wmid_ref, wout_ref, w2_ref, w3_ref):
    eye = one_hot(32, 256, lambda row, lane: row == (lane & 31)).astype(BF)
    for b in range(3):
        blocks = tiled_blocks(wmid_ref, lambda a: 3 * a + b, eye)
        for row_in in range(8):
            start = b * 256 + row_in * 32
            w2_ref[start : start + 32, :] = banded(blocks, row_in, 6)
        blocks = tiled_blocks(wout_ref, lambda a: 3 * a + b, eye[:, :128])
        for row_in in range(8):
            value = banded(blocks, row_in, 4)
            for q in range(2):
                start = (b + q) * 256 + row_in * 32
                w3_ref[start : start + 32, q * 128 : q * 128 + 128] = value
    w3_ref[0:256, 128:256] = jnp.zeros((256, 128), BF)
    w3_ref[768:1024, 0:128] = jnp.zeros((256, 128), BF)


def hidden_weights_kernel(w_ref, ca_ref):
    eye = one_hot(32, 256, lambda row, lane: row == (lane & 31)).astype(BF)
    for plane in range(3):
        for e in range(3):
            blocks = tiled_blocks(w_ref, lambda a: 9 * plane + 3 * a + e, eye)
            for row_in in range(8):
                start = e * 256 + row_in * 32
                ca_ref[plane, start : start + 32, :] = banded(blocks, row_in, 6)


def final_weights_kernel(w_ref, cb_ref):
    eye = one_hot(32, 128, lambda row, lane: row == (lane & 31)).astype(BF)
    blank = jnp.zeros((768, 128), BF)
    cb_ref[0, :, 128:256] = blank
    cb_ref[3, :, 0:128] = blank
    for plane in range(3):
        for e in range(3):
            blocks = tiled_blocks(w_ref, lambda a: 9 * plane + 3 * a + e, eye)
            for row_in in range(8):
                start = e * 256 + row_in * 32
                value = banded(blocks, row_in, 4)
                cb_ref[plane, start : start + 32, 0:128] = value
                cb_ref[plane + 1, start : start + 32, 128:256] = value


def send(value, axis, even, odd):
    count = lax.axis_size(axis)
    pairs = []
    for i in range(count):
        to = i + (odd if i % 2 else even)
        if not 0 <= to < count:
            to = i ^ 1 if abs(even) == 2 else i
        pairs.append((i, to))
    return lax.ppermute(value, axis, pairs)


def swap(value, axis, bit):
    count = lax.axis_size(axis)
    return lax.ppermute(value, axis, [(i, i ^ bit) for i in range(count)])


def limit(mib):
    return pltpu.CompilerParams(vmem_limit_bytes=mib * 1024 * 1024)


def shards(
    images,
    shifts,
    in_weight,
    norm_gain,
    norm_bias,
    mid_weight,
    out_weight,
    cost_weight_a,
    cost_weight_b,
):
    views, rows, colors, width = images.shape
    planes = shifts.shape[1]
    chan = in_weight.shape[2]
    count = lax.axis_size("rows")
    index = lax.axis_index("rows")
    core = index % 2
    total = views * width


    def weights(kernel, shapes, *operands):
        shapes = tuple(jax.ShapeDtypeStruct(shape, BF) for shape in shapes)
        size = 2 * sum(shape.size for shape in shapes)
        return pl.pallas_call(
            kernel,
            name=kernel.__name__,
            out_shape=shapes,
            in_specs=[VMEM] * len(operands),
            out_specs=(VMEM,) * len(shapes),
            cost_estimate=pl.CostEstimate(flops=size, bytes_accessed=2 * size, transcendentals=0),
            compiler_params=limit(8),
        )(*operands)

    own = images.reshape(views, rows * colors, width)
    head, tail = own[:, :colors], own[:, (rows - 1) * colors :]
    pair = swap(own, "rows", 1)
    far = send(own, "rows", -1, 1)
    near = send(jnp.where(core == 0, tail, head), "rows", 2, -2)
    after = send(jnp.where(core == 0, head, tail), "rows", -2, 2)
    colors_in = in_weight.transpose(0, 1, 3, 2).reshape(9 * colors, chan)
    (w1,) = weights(color_weights_kernel, [(128, 384)], colors_in)

    patches, stats = pl.pallas_call(
        stats_kernel,
        name="stats",
        out_shape=(
            jax.ShapeDtypeStruct((total, 128), BF),
            jax.ShapeDtypeStruct((2 * views, 128), F32),
        ),
        in_specs=[VMEM] * 6,
        out_specs=(VMEM, VMEM),
        scratch_shapes=[
            pltpu.VMEM((8, 48, width), F32),
            pltpu.VMEM((8, 128, width), F32),
            pltpu.VMEM(((width + 1) * (views + 1), 128), F32),
        ],
        compiler_params=limit(12),
    )(own, pair, far, near, after, w1)
    jobs = [
        (feature_weights_kernel, [(768, 256), (1024, 256)], (mid_weight.reshape(9, chan, chan), out_weight.reshape(9, chan, chan))),
        (hidden_weights_kernel, [(3, 768, 256)], (cost_weight_a.reshape(27, chan, chan),)),
        (final_weights_kernel, [(4, 768, 256)], (cost_weight_b.reshape(27, chan, chan),)),
    ]
    made, raw = [], []
    bit = 2
    while True:
        last = 2 * bit >= count
        other = swap(stats, "rows", bit)
        last = 2 * bit >= count
        if last or 4 * bit >= count:
            stats, source = lax.optimization_barrier((stats, patches))
            half = pl.pallas_call(
                functools.partial(raw_kernel, len(raw) * (total // 2)),
                name="raw",
                out_shape=jax.ShapeDtypeStruct((total // 2, 384), F32),
                in_specs=[VMEM] * 2,
                out_specs=VMEM,
                cost_estimate=pl.CostEstimate(flops=total * 128 * 384, bytes_accessed=4000000, transcendentals=0),
                compiler_params=limit(8),
            )(source, w1)
            if not last:
                other, half = lax.optimization_barrier((other, half))
            raw.append(half)
        while jobs:
            kernel, shapes, operands = jobs.pop(0)
            if bit > 2:
                stats, operands = lax.optimization_barrier((stats, operands))
            new = weights(kernel, shapes, *operands)
            if not last:
                other, new = lax.optimization_barrier((other, new))
            made.extend(new)
            if not last:
                break
        if last:
            break
        stats = jnp.concatenate(merge(stats, other, views, rows * width * bit), axis=0)
        bit *= 2
    w2, w3, ca, cb = made

    return pl.pallas_call(
        main_kernel,
        name="main",
        out_shape=jax.ShapeDtypeStruct((planes, rows, chan, width), BF),
        in_specs=[SMEM] + [VMEM] * 8 + [pl.BlockSpec(memory_space=pl.ANY)] * 2,
        out_specs=VMEM,
        scratch_shapes=[
            pltpu.VMEM((total + 2 * views, 384), BF),
            pltpu.VMEM((2, total + 2 * views, 256), BF),
            pltpu.VMEM(((2 * width + 1) * (views + 1), 128), F32),
            *[pltpu.VMEM((9, width + 2 * REACH, 128), F32) for _ in range(4)],
            pltpu.VMEM((8, width + 16, 256), F32),
            pltpu.VMEM((planes + 2, width, 768), BF),
            pltpu.VMEM((planes // 2 + 1, 2, width, 768), BF),
            pltpu.VMEM((3, 768, 256), BF),
            pltpu.VMEM((4, 768, 256), BF),
            pltpu.VMEM((8, 128), F32),
            pltpu.SemaphoreType.DMA((2,)),
        ],
        compiler_params=limit(40),
    )(shifts, *raw, stats, other, norm_gain[None], norm_bias[None], w2, w3, ca, cb)


def solution(mesh):
    placed = (P("groups", "rows", None, None), P("groups", None), P(), P(), P(), P(), P(), P(), P())
    return jax.shard_map(
        shards,
        mesh=mesh,
        in_specs=placed,
        out_specs=P("groups", "rows", None, None),
        check_vma=False,
    )
```
